32 devices in a mesh: groups: 2 (over y), chan: 8 (over z, x), pair: 2 (over core).
Axes of the slice: x: 2, y: 2, z: 4, core: 2. Of those that a mesh axis runs over, the one named last changes fastest.
Arguments:
- raw: bfloat16 [1024, 1, 12000], P(('groups', 'chan')), parts along dimension 0, may hold values from -6 to 6
- live_index: int32 [16, 64], P(('groups', 'chan')), parts along dimension 0, may hold values from 0 to 63, each once within a row
- live_count: int32 [16], P('groups'), parts along dimension 0, may hold values from 1 to 64, 256 in all
Outputs:
- correlation: bfloat16 [6, 1024, 512], P('pair', ('groups', 'chan')), parts along dimension 1
The draws below stay inside these ranges and needn't reach their ends.
There are 2 independent parts, one for each index of `groups`. The reference program is written for one: setup_inputs(seed, part) draws one part's arguments, and reference() takes and returns one part's arrays. A program takes and returns all parts, laid end to end along the dimension named above; each array names one. Nothing has to cross between parts.
Inputs may be any that keep to these rules, and one draw needn't show every extreme that they name: `live_index`: each block's row is a permutation of the raw channels of that block. `live_count`: live slots of each block; they sum to 256, and some block fills all 64 slots.
All inputs are finite; a program needn't handle non-finite values.
Results may differ from the reference program's by a relative error of at most 0.001.
The reference program's roundings to bfloat16 on the way (of `picked`, `dft_table`, `whitened` and `weighted`) count: a program that leaves them out, or rounds other values in their place, can miss the bound.
Values may be sent and summed in bfloat16 or wider, within the bound.
A program may use at most 128 MiB of HBM per device.

```python
import math
import jax
import jax.numpy as jnp
import numpy as np
from jax import lax

S = 12000
NB = 448
NSEG = 1
L = 6
LSTEP = 125
F0 = 60
CAP = 64
BLOCKS = 8
SLOTS = 512
LIVE = 256


def level_of(own_key, extent, pieces, least, high):
    gain = 1.0
    for position, shards_of in pieces:
        steps = jax.random.uniform(jax.random.fold_in(jax.random.fold_in(own_key, 6), position), (shards_of,), jnp.float32, least / len(pieces), high / len(pieces))
        gain = gain * jnp.repeat(jnp.exp(steps), extent[position] // shards_of).reshape((-1,) + (1,) * (len(extent) - 1 - position))
    return gain


def split_up(amount, total, most, lean):
    loads = [(1 << 20) // math.isqrt(grade ** lean) + 1 for grade in range(2, amount + 1)]
    spare, holding = total - most - (amount - 1), [1] * (amount - 1)
    while spare > 0:
        candidates = [i for i in range(amount - 1) if holding[i] < most]
        whole, budget = sum([loads[i] for i in candidates]), spare
        for i in candidates:
            extra = min(most - holding[i], max(1, budget * loads[i] // whole), spare)
            holding[i] = holding[i] + extra
            spare = spare - extra
    return np.array([most] + holding)


def uneven_parts(rng, count, total, bound, lean):
    if count == 2:
        one = jax.random.randint(rng, (), max(1, total - bound), min(bound, total - 1) + 1)
        return jnp.stack([one, total - one])
    lengths = jnp.asarray(split_up(count, total, bound, lean), jnp.int32)
    twos = (count - 1) // 2
    source_of, receiver = lengths[1:1 + 2 * twos:2], lengths[2:2 + 2 * twos:2]
    slack = jnp.minimum(source_of - 1, bound - receiver)
    passed = jax.random.randint(jax.random.fold_in(rng, 1), (twos,), 0, 1 << 20) % (slack + 1)
    lengths = lengths.at[1:1 + 2 * twos:2].set(source_of - passed).at[2:2 + 2 * twos:2].set(receiver + passed)
    return lengths[jax.random.permutation(jax.random.fold_in(rng, 2), count)]


def gaussian(key, shape, spread, reach, pieces=(), held_as=jnp.bfloat16):
    drawn = jax.random.normal(key, shape, jnp.float32) * spread
    if len(pieces) > 0:
        drawn = level_of(key, shape, pieces, -0.22, 0.18) * drawn
    return jnp.clip(drawn, min=-reach, max=reach).astype(held_as)


def setup_inputs(seed: int = 0, part: int = 0) -> dict:
    key_list = jax.random.split(jax.random.key(seed), 4)
    part_splits = jax.random.split(jax.random.fold_in(key_list[3], part), 4)
    raw = gaussian(part_splits[0], (SLOTS, NSEG, S), 1.0, 6.0, ((0, 8),))
    live_index = jax.vmap(lambda own: jax.random.permutation(own, CAP))(jax.random.split(part_splits[1], BLOCKS)).reshape((BLOCKS, CAP)).astype(jnp.int32)
    live_count = uneven_parts(part_splits[2], BLOCKS, LIVE, CAP, 2).astype(jnp.int32)
    return dict(raw=raw, live_index=live_index, live_count=live_count)


water_level = 0.1

def lag_weights(lag_ids, bin_ids):
    band_taper = 0.5 - 0.5 * jnp.cos(2.0 * jnp.pi * (bin_ids.astype(jnp.float32) + 0.5) / NB)
    phase_int = (F0 + bin_ids)[None, :] * lag_ids[:, None] % S
    waves = jnp.cos(phase_int.astype(jnp.float32) * (2.0 * jnp.pi / S))
    return band_taper[None, :] * waves / jnp.sqrt(jnp.float32(NSEG * NB))

def reference(raw, live_index, live_count):
    blocks = live_count.shape[0]
    raw_rows = (jnp.arange(blocks, dtype=jnp.int32)[:, None] * CAP + live_index).reshape(-1).astype(jnp.int32)
    live_mask = (jnp.arange(CAP, dtype=jnp.int32)[None, :] < live_count[:, None]).reshape(-1)
    picked = jnp.where(live_mask[:, None, None], raw[raw_rows], jnp.zeros((), raw.dtype))
    sample_ids = jnp.arange(S, dtype=jnp.int32)
    bin_ids = jnp.arange(NB, dtype=jnp.int32)
    phase_int = sample_ids[:, None] * (F0 + bin_ids)[None, :] % S
    angles = phase_int.astype(jnp.float32) * (2.0 * jnp.pi / S)
    dft_table = jnp.concatenate([jnp.cos(angles), -jnp.sin(angles)], axis=1).astype(jnp.bfloat16)
    spectrum = jnp.dot(picked.reshape(-1, S), dft_table, preferred_element_type=jnp.float32)
    spectrum = spectrum.reshape(SLOTS, NSEG, 2, NB)
    band_power = lax.optimization_barrier(jnp.sum(spectrum * spectrum, axis=(2, 3))) / NB
    magnitude = spectrum[:, :, 0] ** 2 + spectrum[:, :, 1] ** 2
    denom = jnp.sqrt(magnitude + water_level * band_power[:, :, None] + 1e-06)
    whitened = (spectrum / denom[:, :, None, :]).astype(jnp.bfloat16)
    flat_spectra = whitened.reshape(SLOTS, -1)
    lag_ids = (jnp.arange(L, dtype=jnp.int32) * LSTEP).astype(jnp.int32)
    weights = lag_weights(lag_ids, bin_ids)

    def per_lag(weight_row):
        weighted = (whitened.astype(jnp.float32) * weight_row[None, None, None, :]).astype(jnp.bfloat16)
        product = lax.dot_general(weighted.reshape(SLOTS, -1), flat_spectra, (((1,), (1,)), ((), ())), preferred_element_type=jnp.float32)
        return product.astype(jnp.bfloat16)
    return lax.map(per_lag, weights)
```

```python
import functools

import jax
import jax.numpy as jnp
import numpy as np
from jax import lax
from jax.experimental import pallas as pl
from jax.experimental.pallas import tpu as pltpu
from jax.sharding import PartitionSpec as P

S = 12000
NB = 448
L = 6
LSTEP = 125
F0 = 60
WATER = 0.1
QUARTER = S // 4
BASE = 128
PAIRS = 5
MADE = 2 * BASE * PAIRS
KROWS = 3072
TROWS = 3008
FULL = NB // 128
TAIL = NB - 128 * FULL
COLS = 2 * NB
VMEM_LIMIT = 63_300_000


def column_bins():
    full = np.arange(128 * FULL).reshape(FULL, 1, 128)
    tail = np.arange(128 * FULL, NB)
    return np.concatenate([np.repeat(full, 2, axis=1).reshape(-1), tail, tail])


def column_is_sine():
    full = np.repeat(np.arange(2) == 1, 128)
    return np.concatenate([np.tile(full, FULL), np.repeat(np.arange(2) == 1, TAIL)])


def dft_table():
    phase = np.arange(MADE, QUARTER)[:, None] * (F0 + column_bins())[None, :] % S
    angle = (phase.astype(np.float32) * np.float32(2.0 * np.pi / S)).astype(np.float64)
    out = np.zeros((TROWS - MADE, COLS), np.float32)
    out[: QUARTER - MADE] = np.where(column_is_sine()[None, :], -np.sin(angle), np.cos(angle))
    return out


def rotations(steps, shift=0.0):
    phase = np.asarray(steps)[:, None] * (F0 + column_bins())[None, :] % S
    angle = 2.0 * np.pi * phase / S + shift
    return np.cos(angle), -np.sin(angle)


def rotation_table():
    step = 2.0 * np.pi / S
    shift = np.pi * (float(np.float32(step)) / step - 1.0)
    sine = column_is_sine()[None, :]
    c, s = rotations(np.arange(BASE) + BASE * PAIRS - BASE // 2, shift)
    base = np.concatenate([np.where(sine, s, c), np.where(sine, c, s)[:, -128:]], axis=1)
    c, s = rotations(BASE // 2 * (2 * np.arange(PAIRS) + 1))
    c[:, 128:256], c[:, 384:512], c[:, 640:768] = s[:, :128], s[:, 256:384], s[:, 512:640]
    turns = np.concatenate([c, np.where(sine, s, -s)[:, -128:]], axis=1)
    return np.concatenate([base, np.repeat(turns, 8, axis=0)], axis=0).astype(np.float32)


def lag_table():
    j = column_bins()
    taper = 0.5 - 0.5 * np.cos(2.0 * np.pi * (j + 0.5) / NB)
    lags = np.arange(L)[:, None] * LSTEP
    waves = np.cos(2.0 * np.pi * (((F0 + j)[None, :] * lags) % S) / S)
    table = np.zeros((2, 8, COLS), np.float32)
    table[:, : L // 2] = (taper[None, :] * waves / np.sqrt(NB)).reshape(2, L // 2, COLS)
    return table.reshape(16, COLS)


def make_rows(rot_ref, table_ref):
    def pair(m, carry):
        turn_rows = pl.ds(pl.multiple_of(BASE + 8 * m, 8), 8)
        above = pl.multiple_of(BASE * (PAIRS + m), BASE)
        below = pl.multiple_of(BASE * (PAIRS - 1 - m), BASE)
        for v in range(FULL + 1):
            one, two = slice(256 * v, 256 * v + 128), slice(256 * v + 128, 256 * v + 256)
            turn_c = jnp.concatenate([rot_ref[turn_rows, one]] * 2, axis=0)
            turn_s = jnp.concatenate([rot_ref[turn_rows, two]] * 2, axis=0)
            for r in range(0, BASE, 16):
                c, s = rot_ref[r : r + 16, one], rot_ref[r : r + 16, two]
                cc, ss = c * turn_c, s * turn_s
                up, down = pl.ds(above + r, 16), pl.ds(below + r, 16)
                if v < FULL:
                    sc, cs = s * turn_c, c * turn_s
                    table_ref[up, one] = (cc - ss).astype(jnp.bfloat16)
                    table_ref[down, one] = (cc + ss).astype(jnp.bfloat16)
                    table_ref[up, two] = (sc + cs).astype(jnp.bfloat16)
                    table_ref[down, two] = (sc - cs).astype(jnp.bfloat16)
                else:
                    table_ref[up, one] = (cc + ss).astype(jnp.bfloat16)
                    table_ref[down, one] = (cc - ss).astype(jnp.bfloat16)
        return carry

    lax.fori_loop(0, PAIRS, pair, 0)


def lane_signs(slots, first):
    m = (lax.broadcasted_iota(jnp.int32, (slots, 128), 1) + first) % 4
    return m % 2 == 0, jnp.where(m < 2, 1.0, -1.0)


def combine(spec, slots):
    a = [spec[slots * q : slots * (q + 1), 0:128] for q in range(4)]
    b = [spec[slots * q : slots * (q + 1), 128:256] for q in range(4)]
    even, sign = lane_signs(slots, F0)
    re = jnp.where(even, a[0] + a[2] + sign * (a[1] + a[3]), a[0] - a[2] + sign * (b[1] - b[3]))
    im = jnp.where(even, b[0] + b[2] + sign * (b[1] + b[3]), b[0] - b[2] - sign * (a[1] - a[3]))
    return re, im


def combine_tail(spec, slots):
    v = [spec[slots * q : slots * (q + 1), :] for q in range(4)]
    even, sign = lane_signs(slots, F0)
    real = lax.broadcasted_iota(jnp.int32, (slots, 128), 1) < TAIL
    turned = jnp.where(real, sign, -sign) * pltpu.roll(v[1] - v[3], TAIL, 1)
    return jnp.where(even, v[0] + v[2] + sign * (v[1] + v[3]), v[0] - v[2] + turned)


def kernel(
    n,
    raw_hbm,
    index_hbm,
    count_hbm,
    rot_hbm,
    table_hbm,
    lag_hbm,
    out_ref,
    index_ref,
    count_ref,
    lag_ref,
    rot_ref,
    x_ref,
    xq_ref,
    table_ref,
    spec_ref,
    spread_ref,
    lagged_ref,
    load_sem,
    rot_sem,
    small_sem,
    table_sem,
    zsend_sem,
    zrecv_sem,
    xsend_sem,
    xrecv_sem,
    fsend_sem,
    frecv_sem,
):
    slots = raw_hbm.shape[0]
    half = slots // 2
    me = lax.axis_index("chan")
    core = lax.axis_index("pair")
    other = 1 - core

    rot_load = pltpu.make_async_copy(rot_hbm, rot_ref, rot_sem)
    rot_load.start()
    load = pltpu.make_async_copy(raw_hbm, x_ref, load_sem)
    load.start()
    small_loads = [
        pltpu.make_async_copy(index_hbm, index_ref, small_sem.at[0]),
        pltpu.make_async_copy(count_hbm, count_ref, small_sem.at[1]),
        pltpu.make_async_copy(lag_hbm, lag_ref, small_sem.at[2]),
    ]
    table_load = pltpu.make_async_copy(table_hbm, table_ref.at[MADE:TROWS], table_sem)
    for small in small_loads:
        small.start()
    table_load.start()

    lines = n // 2
    line, side = me // 2, lax.rem(me, 2)
    mate = 2 * line + 1 - side
    order = list(range(1, lines))

    def chip(d, which):
        row = line
        for bit in range(lines.bit_length()):
            if d >> bit & 1:
                row = row + (1 << bit) - (2 << bit) * (line // (1 << bit) % 2)
        return 2 * row + which

    barrier = pltpu.get_barrier_semaphore()
    pl.semaphore_signal(barrier, inc=1, device_id={"pair": other})
    pl.semaphore_signal(barrier, inc=1, device_id={"chan": mate})
    for d in order:
        pl.semaphore_signal(barrier, inc=1, device_id={"chan": chip(d, side)})

    rot_load.wait()
    make_rows(rot_ref, table_ref)
    table_ref[TROWS:, :] = jnp.zeros((KROWS - TROWS, COLS), jnp.bfloat16)
    load.wait()
    for q in range(4):
        rows = slice(slots * q, slots * (q + 1))
        xq_ref[rows, 0:QUARTER] = x_ref[:, QUARTER * q : QUARTER * (q + 1)]
        xq_ref[rows, QUARTER:] = jnp.zeros((slots, KROWS - QUARTER), jnp.bfloat16)

    spectrum = jnp.dot(xq_ref[:, :MADE], table_ref[:MADE, :], preferred_element_type=jnp.float32)
    spec_ref[...] = spectrum
    table_load.wait()
    spectrum = spec_ref[...] + jnp.dot(
        xq_ref[:, MADE:], table_ref[MADE:, :], preferred_element_type=jnp.float32
    )

    parts, power = [], jnp.zeros((slots, 1), jnp.float32)
    for j in range(FULL + 1):
        spec = spectrum[:, 256 * j : 256 * j + 256]
        if j < FULL:
            re, im = combine(spec, slots)
            mag = re * re + im * im
            power = power + jnp.sum(mag, axis=1, keepdims=True)
        else:
            both = combine_tail(spec, slots)
            square = both * both
            mag = square + pltpu.roll(square, TAIL, 1)
            power = power + jnp.sum(square, axis=1, keepdims=True)
        parts.append((re, im, mag) if j < FULL else (both, None, mag))
    floor = power * (WATER / NB) + 1e-06
    whitened = []
    for re, im, mag in parts:
        scale = lax.rsqrt(mag + floor)
        whitened.append(re * scale)
        if im is not None:
            whitened.append(im * scale)
    whitened = jnp.concatenate(whitened, axis=1).astype(jnp.bfloat16)

    for small in small_loads:
        small.wait()
    r_ids = lax.broadcasted_iota(jnp.int32, (slots, slots), 0)
    k_ids = lax.broadcasted_iota(jnp.int32, (slots, slots), 1)
    chosen = (index_ref[...] == r_ids) & (k_ids < count_ref[me])
    pick = jnp.where(chosen, 1.0, 0.0).T.astype(jnp.bfloat16)
    own = jnp.dot(pick, whitened, preferred_element_type=jnp.float32)
    own16 = own.astype(jnp.bfloat16)
    spread_ref[pl.ds(pl.multiple_of(me * slots, slots), slots), :] = own16

    def part(block, who):
        return spread_ref.at[pl.ds(pl.multiple_of(block * slots + who * half, half), half), :]

    pl.semaphore_wait(barrier, lines + 1)

    def copy(block, who, sends, recvs, at, device_id):
        ref = part(block, who)
        return pltpu.make_async_remote_copy(
            src_ref=ref,
            dst_ref=ref,
            send_sem=sends.at[at],
            recv_sem=recvs.at[at],
            device_id=device_id,
        )

    def along(d, block):
        return copy(block, core, zsend_sem, zrecv_sem, d, {"chan": chip(d, side)})

    def across(d, which):
        return copy(chip(d, which), core, xsend_sem, xrecv_sem, d, {"chan": mate})

    def inside(d, which, who):
        at = d + lines * (1 if which is side else 0)
        return copy(chip(d, which), who, fsend_sem, frecv_sem, at, {"pair": other})

    far = 1 - side
    across(0, side).start()
    for d in order:
        along(d, me).start()
    weights = lag_ref[pl.ds(pl.multiple_of(8 * core, 8), 8), :]
    for l in range(L // 2):
        weight = weights[l : l + 1, :]
        lagged_ref[slots * l : slots * (l + 1), :] = (own * weight).astype(jnp.bfloat16)

    across(0, far).wait_recv()
    inside(0, far, core).start()
    for d in order:
        along(d, chip(d, side)).wait_recv()
        across(d, side).start()
        inside(d, side, core).start()

    for i, d in enumerate([0] + order):
        if d > 0:
            across(d, far).wait_recv()
            inside(d, far, core).start()
            inside(d, side, other).wait_recv()
        inside(d, far, other).wait_recv()
        at = pl.multiple_of(chip(d, 0) * slots, 2 * slots)
        product = lax.dot_general(
            lagged_ref[...],
            spread_ref[pl.ds(at, 2 * slots), :],
            (((1,), (1,)), ((), ())),
            preferred_element_type=jnp.float32,
        ).astype(jnp.bfloat16)
        for l in range(L // 2):
            out_ref[l, :, pl.ds(at, 2 * slots)] = product[slots * l : slots * (l + 1)]

    for d in [0] + order:
        across(d, side).wait_send()
        inside(d, far, core).wait_send()
        if d > 0:
            along(d, me).wait_send()
            inside(d, side, core).wait_send()


def shards(n, raw, live_index, live_count):
    slots = raw.shape[0]
    vmem = pl.BlockSpec(memory_space=pltpu.VMEM)
    return pl.pallas_call(
        functools.partial(kernel, n),
        out_shape=pltpu.VMEM((L // 2, slots, n * slots), jnp.bfloat16),
        in_specs=[
            pl.BlockSpec(memory_space=pl.ANY),
            pl.BlockSpec(memory_space=pl.ANY),
            pl.BlockSpec(memory_space=pl.ANY),
            pl.BlockSpec(memory_space=pl.ANY),
            pl.BlockSpec(memory_space=pl.ANY),
            pl.BlockSpec(memory_space=pl.ANY),
        ],
        out_specs=vmem,
        scratch_shapes=[
            pltpu.VMEM((1, slots), jnp.int32),
            pltpu.SMEM((n,), jnp.int32),
            pltpu.VMEM((16, COLS), jnp.float32),
            pltpu.VMEM((BASE + 8 * PAIRS, COLS + 128), jnp.float32),
            pltpu.VMEM((slots, S), jnp.bfloat16),
            pltpu.VMEM((4 * slots, KROWS), jnp.bfloat16),
            pltpu.VMEM((KROWS, COLS), jnp.bfloat16),
            pltpu.VMEM((4 * slots, COLS), jnp.float32),
            pltpu.VMEM((n * slots, COLS), jnp.bfloat16),
            pltpu.VMEM((L // 2 * slots, COLS), jnp.bfloat16),
            pltpu.SemaphoreType.DMA,
            pltpu.SemaphoreType.DMA,
            pltpu.SemaphoreType.DMA((3,)),
            pltpu.SemaphoreType.DMA,
            pltpu.SemaphoreType.DMA((n // 2,)),
            pltpu.SemaphoreType.DMA((n // 2,)),
            pltpu.SemaphoreType.DMA((n // 2,)),
            pltpu.SemaphoreType.DMA((n // 2,)),
            pltpu.SemaphoreType.DMA((n,)),
            pltpu.SemaphoreType.DMA((n,)),
        ],
        compiler_params=pltpu.CompilerParams(
            collective_id=0, has_side_effects=True, vmem_limit_bytes=VMEM_LIMIT - 6 * slots * n * slots
        ),
    )(
        raw.reshape(slots, S),
        live_index,
        live_count,
        jnp.asarray(rotation_table()),
        jnp.asarray(dft_table(), jnp.bfloat16),
        jnp.asarray(lag_table()),
    )


def solution(mesh):
    return jax.shard_map(
        functools.partial(shards, mesh.shape["chan"]),
        mesh=mesh,
        in_specs=(P(("groups", "chan"), None, None), P(("groups", "chan"), None), P("groups")),
        out_specs=P("pair", ("groups", "chan"), None),
        check_vma=False,
    )
```

```python
import functools

import jax
import jax.numpy as jnp
import numpy as np
from jax import lax
from jax.experimental import pallas as pl
from jax.experimental.pallas import tpu as pltpu
from jax.sharding import PartitionSpec as P

S = 12000
NB = 448
L = 6
LSTEP = 125
F0 = 60
WATER = 0.1
QUARTER = S // 4
BASE = 128
PAIRS = 5
MADE = 2 * BASE * PAIRS
KROWS = 3072
PIECES = 2
TROWS = 3008
FULL = NB // 128
TAIL = NB - 128 * FULL
COLS = 2 * NB
VMEM_LIMIT = 63_300_000


def column_bins():
    full = np.arange(128 * FULL).reshape(FULL, 1, 128)
    tail = np.arange(128 * FULL, NB)
    return np.concatenate([np.repeat(full, 2, axis=1).reshape(-1), tail, tail])


def column_is_sine():
    full = np.repeat(np.arange(2) == 1, 128)
    return np.concatenate([np.tile(full, FULL), np.repeat(np.arange(2) == 1, TAIL)])


def dft_table():
    phase = np.arange(MADE, QUARTER)[:, None] * (F0 + column_bins())[None, :] % S
    angle = (phase.astype(np.float32) * np.float32(2.0 * np.pi / S)).astype(np.float64)
    out = np.zeros((TROWS - MADE, COLS), np.float32)
    out[: QUARTER - MADE] = np.where(column_is_sine()[None, :], -np.sin(angle), np.cos(angle))
    return out


def rotations(steps, shift=0.0):
    phase = np.asarray(steps)[:, None] * (F0 + column_bins())[None, :] % S
    angle = 2.0 * np.pi * phase / S + shift
    return np.cos(angle), -np.sin(angle)


def rotation_table():
    step = 2.0 * np.pi / S
    shift = np.pi * (float(np.float32(step)) / step - 1.0)
    sine = column_is_sine()[None, :]
    c, s = rotations(np.arange(BASE) + BASE * PAIRS - BASE // 2, shift)
    base = np.concatenate([np.where(sine, s, c), np.where(sine, c, s)[:, -128:]], axis=1)
    c, s = rotations(BASE // 2 * (2 * np.arange(PAIRS) + 1))
    c[:, 128:256], c[:, 384:512], c[:, 640:768] = s[:, :128], s[:, 256:384], s[:, 512:640]
    turns = np.concatenate([c, np.where(sine, s, -s)[:, -128:]], axis=1)
    return np.concatenate([base, np.repeat(turns, 8, axis=0)], axis=0).astype(np.float32)


def lag_table():
    j = column_bins()
    taper = 0.5 - 0.5 * np.cos(2.0 * np.pi * (j + 0.5) / NB)
    lags = np.arange(L)[:, None] * LSTEP
    waves = np.cos(2.0 * np.pi * (((F0 + j)[None, :] * lags) % S) / S)
    table = np.zeros((2, 8, COLS), np.float32)
    table[:, : L // 2] = (taper[None, :] * waves / np.sqrt(NB)).reshape(2, L // 2, COLS)
    return table.reshape(16, COLS)


def make_rows(rot_ref, table_ref):
    def pair(m, carry):
        turn_rows = pl.ds(pl.multiple_of(BASE + 8 * m, 8), 8)
        above = pl.multiple_of(BASE * (PAIRS + m), BASE)
        below = pl.multiple_of(BASE * (PAIRS - 1 - m), BASE)
        for v in range(FULL + 1):
            one, two = slice(256 * v, 256 * v + 128), slice(256 * v + 128, 256 * v + 256)
            turn_c = jnp.concatenate([rot_ref[turn_rows, one]] * 2, axis=0)
            turn_s = jnp.concatenate([rot_ref[turn_rows, two]] * 2, axis=0)
            for r in range(0, BASE, 16):
                c, s = rot_ref[r : r + 16, one], rot_ref[r : r + 16, two]
                cc, ss = c * turn_c, s * turn_s
                up, down = pl.ds(above + r, 16), pl.ds(below + r, 16)
                if v < FULL:
                    sc, cs = s * turn_c, c * turn_s
                    table_ref[up, one] = (cc - ss).astype(jnp.bfloat16)
                    table_ref[down, one] = (cc + ss).astype(jnp.bfloat16)
                    table_ref[up, two] = (sc + cs).astype(jnp.bfloat16)
                    table_ref[down, two] = (sc - cs).astype(jnp.bfloat16)
                else:
                    table_ref[up, one] = (cc + ss).astype(jnp.bfloat16)
                    table_ref[down, one] = (cc - ss).astype(jnp.bfloat16)
        return carry

    lax.fori_loop(0, PAIRS, pair, 0)


def lane_signs(slots, first):
    m = (lax.broadcasted_iota(jnp.int32, (slots, 128), 1) + first) % 4
    return m % 2 == 0, jnp.where(m < 2, 1.0, -1.0)


def combine(spec, slots):
    a = [spec[slots * q : slots * (q + 1), 0:128] for q in range(4)]
    b = [spec[slots * q : slots * (q + 1), 128:256] for q in range(4)]
    even, sign = lane_signs(slots, F0)
    re = jnp.where(even, a[0] + a[2] + sign * (a[1] + a[3]), a[0] - a[2] + sign * (b[1] - b[3]))
    im = jnp.where(even, b[0] + b[2] + sign * (b[1] + b[3]), b[0] - b[2] - sign * (a[1] - a[3]))
    return re, im


def combine_tail(spec, slots):
    v = [spec[slots * q : slots * (q + 1), :] for q in range(4)]
    even, sign = lane_signs(slots, F0)
    real = lax.broadcasted_iota(jnp.int32, (slots, 128), 1) < TAIL
    turned = jnp.where(real, sign, -sign) * pltpu.roll(v[1] - v[3], TAIL, 1)
    return jnp.where(even, v[0] + v[2] + sign * (v[1] + v[3]), v[0] - v[2] + turned)


def kernel(
    n,
    raw_hbm,
    index_hbm,
    count_hbm,
    rot_hbm,
    table_hbm,
    lag_hbm,
    out_ref,
    index_ref,
    count_ref,
    lag_ref,
    rot_ref,
    x_ref,
    xq_ref,
    table_ref,
    spec_ref,
    spread_ref,
    lagged_ref,
    load_sem,
    rot_sem,
    small_sem,
    table_sem,
    far_send,
    far_recv,
    near_send,
    near_recv,
    in_send,
    in_recv,
):
    slots = raw_hbm.shape[0]
    half = slots // 2
    me = lax.axis_index("chan")
    core = lax.axis_index("pair")
    other = 1 - core

    rot_load = pltpu.make_async_copy(rot_hbm, rot_ref, rot_sem)
    rot_load.start()
    load = pltpu.make_async_copy(raw_hbm, x_ref, load_sem)
    load.start()
    small_loads = [
        pltpu.make_async_copy(index_hbm, index_ref, small_sem.at[0]),
        pltpu.make_async_copy(count_hbm, count_ref, small_sem.at[1]),
        pltpu.make_async_copy(lag_hbm, lag_ref, small_sem.at[2]),
    ]
    table_load = pltpu.make_async_copy(table_hbm, table_ref.at[MADE:TROWS], table_sem)
    for small in small_loads:
        small.start()
    table_load.start()

    quads = n // 4
    quad, corner = me // 4, lax.rem(me, 4)
    fars = list(range(1, quads))

    def flip(value, mask):
        for bit in range(mask.bit_length()):
            if mask >> bit & 1:
                value = value + (1 << bit) - (2 << bit) * lax.rem(value // (1 << bit), 2)
        return value

    def chip(f, e):
        return 4 * flip(quad, f) + flip(corner, e)

    barrier = pltpu.get_barrier_semaphore()
    pl.semaphore_signal(barrier, inc=1, device_id={"pair": other})
    for e in (1, 2, 3):
        pl.semaphore_signal(barrier, inc=1, device_id={"chan": chip(0, e)})

    @pl.when(core == 1)
    def _():
        for f in fars:
            pl.semaphore_signal(barrier, inc=1, device_id={"chan": chip(f, 0)})

    rot_load.wait()
    make_rows(rot_ref, table_ref)
    table_ref[TROWS:, :] = jnp.zeros((KROWS - TROWS, COLS), jnp.bfloat16)
    load.wait()
    for q in range(4):
        rows = slice(slots * q, slots * (q + 1))
        xq_ref[rows, 0:QUARTER] = x_ref[:, QUARTER * q : QUARTER * (q + 1)]
        xq_ref[rows, QUARTER:] = jnp.zeros((slots, KROWS - QUARTER), jnp.bfloat16)

    spectrum = jnp.dot(xq_ref[:, :MADE], table_ref[:MADE, :], preferred_element_type=jnp.float32)
    spec_ref[...] = spectrum
    table_load.wait()
    spectrum = spec_ref[...] + jnp.dot(
        xq_ref[:, MADE:], table_ref[MADE:, :], preferred_element_type=jnp.float32
    )

    parts, power = [], jnp.zeros((slots, 1), jnp.float32)
    for j in range(FULL + 1):
        spec = spectrum[:, 256 * j : 256 * j + 256]
        if j < FULL:
            re, im = combine(spec, slots)
            mag = re * re + im * im
            power = power + jnp.sum(mag, axis=1, keepdims=True)
        else:
            both = combine_tail(spec, slots)
            square = both * both
            mag = square + pltpu.roll(square, TAIL, 1)
            power = power + jnp.sum(square, axis=1, keepdims=True)
        parts.append((re, im, mag) if j < FULL else (both, None, mag))
    floor = power * (WATER / NB) + 1e-06
    whitened = []
    for re, im, mag in parts:
        scale = lax.rsqrt(mag + floor)
        whitened.append(re * scale)
        if im is not None:
            whitened.append(im * scale)
    whitened = jnp.concatenate(whitened, axis=1).astype(jnp.bfloat16)

    for small in small_loads:
        small.wait()
    r_ids = lax.broadcasted_iota(jnp.int32, (slots, slots), 0)
    k_ids = lax.broadcasted_iota(jnp.int32, (slots, slots), 1)
    chosen = (index_ref[...] == r_ids) & (k_ids < count_ref[me])
    pick = jnp.where(chosen, 1.0, 0.0).T.astype(jnp.bfloat16)
    own = jnp.dot(pick, whitened, preferred_element_type=jnp.float32)
    own16 = own.astype(jnp.bfloat16)
    spread_ref[pl.ds(pl.multiple_of(me * slots, slots), slots), :] = own16

    def copy(block, first, rows, sends, recvs, at, device_id):
        ref = spread_ref.at[pl.ds(pl.multiple_of(block * slots + first, rows), rows), :]
        return pltpu.make_async_remote_copy(
            src_ref=ref,
            dst_ref=ref,
            send_sem=sends.at[at],
            recv_sem=recvs.at[at],
            device_id=device_id,
        )

    part = slots // PIECES

    def far(f, i, block):
        return copy(block, part * i, part, far_send, far_recv, f * PIECES + i, {"chan": chip(f, 0)})

    def near(f, e, i, block):
        at = (4 * f + e) * PIECES + i
        return copy(block, part * i, part, near_send, near_recv, at, {"chan": chip(0, e)})

    def inside(f, e, i):
        at = (4 * f + e) * PIECES + i
        return copy(chip(f, e), part * i, part, in_send, in_recv, at, {"pair": other})

    def mine(e):
        return copy(me, 0, slots, near_send, near_recv, e * PIECES, {"chan": chip(0, e)})

    def mates(e):
        return copy(chip(0, e), 0, slots, in_send, in_recv, e * PIECES, {"pair": other})

    def lag_rows():
        weights = lag_ref[pl.ds(pl.multiple_of(8 * core, 8), 8), :]
        for l in range(L // 2):
            weight = weights[l : l + 1, :]
            lagged_ref[slots * l : slots * (l + 1), :] = (own * weight).astype(jnp.bfloat16)

    def correlate(f, e):
        at = pl.multiple_of(chip(f, e) // 2 * 2 * slots, 2 * slots)
        product = lax.dot_general(
            lagged_ref[...],
            spread_ref[pl.ds(at, 2 * slots), :],
            (((1,), (1,)), ((), ())),
            preferred_element_type=jnp.float32,
        ).astype(jnp.bfloat16)
        for l in range(L // 2):
            out_ref[l, :, pl.ds(at, 2 * slots)] = product[slots * l : slots * (l + 1)]

    pieces = range(PIECES)

    @pl.when(core == 0)
    def _():
        pl.semaphore_wait(barrier, 4)
        for e in (1, 3, 2):
            mine(e).start()
        lag_rows()
        for e in (1, 3, 2):
            mine(e).wait_recv()
            mates(e).start()
        correlate(0, 0)
        correlate(0, 2)
        for f in fars:
            for pair in ((0, 1), (2, 3)):
                for e in pair:
                    for i in pieces:
                        inside(f, e, i).wait_recv()
                correlate(f, pair[0])
        for e in (1, 3, 2):
            mine(e).wait_send()
            mates(e).wait_send()

    @pl.when(core == 1)
    def _():
        pl.semaphore_wait(barrier, quads + 3)
        for f in fars:
            for i in pieces:
                far(f, i, me).start()
        lag_rows()
        for f in fars:
            for i in pieces:
                far(f, i, me).wait_recv()
                for e in (3, 2, 1):
                    near(f, e, i, chip(f, 0)).start()
                inside(f, 0, i).start()
        for f in fars:
            for i in pieces:
                for e in (1, 2, 3):
                    near(f, e, i, me).wait_recv()
                    inside(f, e, i).start()
            correlate(f, 0)
            correlate(f, 2)
        for e in (1, 3, 2):
            mates(e).wait_recv()
        correlate(0, 0)
        correlate(0, 2)
        for f in fars:
            for i in pieces:
                far(f, i, me).wait_send()
                inside(f, 0, i).wait_send()
                for e in (1, 2, 3):
                    near(f, e, i, me).wait_send()
                    inside(f, e, i).wait_send()


def shards(n, raw, live_index, live_count):
    slots = raw.shape[0]
    vmem = pl.BlockSpec(memory_space=pltpu.VMEM)
    return pl.pallas_call(
        functools.partial(kernel, n),
        out_shape=pltpu.VMEM((L // 2, slots, n * slots), jnp.bfloat16),
        in_specs=[
            pl.BlockSpec(memory_space=pl.ANY),
            pl.BlockSpec(memory_space=pl.ANY),
            pl.BlockSpec(memory_space=pl.ANY),
            pl.BlockSpec(memory_space=pl.ANY),
            pl.BlockSpec(memory_space=pl.ANY),
            pl.BlockSpec(memory_space=pl.ANY),
        ],
        out_specs=vmem,
        scratch_shapes=[
            pltpu.VMEM((1, slots), jnp.int32),
            pltpu.SMEM((n,), jnp.int32),
            pltpu.VMEM((16, COLS), jnp.float32),
            pltpu.VMEM((BASE + 8 * PAIRS, COLS + 128), jnp.float32),
            pltpu.VMEM((slots, S), jnp.bfloat16),
            pltpu.VMEM((4 * slots, KROWS), jnp.bfloat16),
            pltpu.VMEM((KROWS, COLS), jnp.bfloat16),
            pltpu.VMEM((4 * slots, COLS), jnp.float32),
            pltpu.VMEM((n * slots, COLS), jnp.bfloat16),
            pltpu.VMEM((L // 2 * slots, COLS), jnp.bfloat16),
            pltpu.SemaphoreType.DMA,
            pltpu.SemaphoreType.DMA,
            pltpu.SemaphoreType.DMA((3,)),
            pltpu.SemaphoreType.DMA,
            pltpu.SemaphoreType.DMA((n // 4 * PIECES,)),
            pltpu.SemaphoreType.DMA((n // 4 * PIECES,)),
            pltpu.SemaphoreType.DMA((n * PIECES,)),
            pltpu.SemaphoreType.DMA((n * PIECES,)),
            pltpu.SemaphoreType.DMA((n * PIECES,)),
            pltpu.SemaphoreType.DMA((n * PIECES,)),
        ],
        compiler_params=pltpu.CompilerParams(
            collective_id=0, has_side_effects=True, vmem_limit_bytes=VMEM_LIMIT - 6 * slots * n * slots
        ),
    )(
        raw.reshape(slots, S),
        live_index,
        live_count,
        jnp.asarray(rotation_table()),
        jnp.asarray(dft_table(), jnp.bfloat16),
        jnp.asarray(lag_table()),
    )


def solution(mesh):
    return jax.shard_map(
        functools.partial(shards, mesh.shape["chan"]),
        mesh=mesh,
        in_specs=(P(("groups", "chan"), None, None), P(("groups", "chan"), None), P("groups")),
        out_specs=P("pair", ("groups", "chan"), None),
        check_vma=False,
    )
```

```python
import functools

import jax
import jax.numpy as jnp
import numpy as np
from jax import lax
from jax.experimental import pallas as pl
from jax.experimental.pallas import tpu as pltpu
from jax.sharding import PartitionSpec as P

S = 12000
NB = 448
L = 6
LSTEP = 125
F0 = 60
WATER = 0.1
QUARTER = S // 4
BASE = 128
PAIRS = 5
MADE = 2 * BASE * PAIRS
KROWS = 3072
TROWS = 3008
FULL = NB // 128
TAIL = NB - 128 * FULL
COLS = 2 * NB
VMEM_LIMIT = 63_300_000


def column_bins():
    full = np.arange(128 * FULL).reshape(FULL, 1, 128)
    tail = np.arange(128 * FULL, NB)
    return np.concatenate([np.repeat(full, 2, axis=1).reshape(-1), tail, tail])


def column_is_sine():
    full = np.repeat(np.arange(2) == 1, 128)
    return np.concatenate([np.tile(full, FULL), np.repeat(np.arange(2) == 1, TAIL)])


def dft_table():
    phase = np.arange(MADE, QUARTER)[:, None] * (F0 + column_bins())[None, :] % S
    angle = (phase.astype(np.float32) * np.float32(2.0 * np.pi / S)).astype(np.float64)
    out = np.zeros((TROWS - MADE, COLS), np.float32)
    out[: QUARTER - MADE] = np.where(column_is_sine()[None, :], -np.sin(angle), np.cos(angle))
    return out


def rotations(steps, shift=0.0):
    phase = np.asarray(steps)[:, None] * (F0 + column_bins())[None, :] % S
    angle = 2.0 * np.pi * phase / S + shift
    return np.cos(angle), -np.sin(angle)


def rotation_table():
    step = 2.0 * np.pi / S
    shift = np.pi * (float(np.float32(step)) / step - 1.0)
    sine = column_is_sine()[None, :]
    c, s = rotations(np.arange(BASE) + BASE * PAIRS - BASE // 2, shift)
    base = np.concatenate([np.where(sine, s, c), np.where(sine, c, s)[:, -128:]], axis=1)
    c, s = rotations(BASE // 2 * (2 * np.arange(PAIRS) + 1))
    c[:, 128:256], c[:, 384:512], c[:, 640:768] = s[:, :128], s[:, 256:384], s[:, 512:640]
    turns = np.concatenate([c, np.where(sine, s, -s)[:, -128:]], axis=1)
    return np.concatenate([base, np.repeat(turns, 8, axis=0)], axis=0).astype(np.float32)


def lag_table():
    j = column_bins()
    taper = 0.5 - 0.5 * np.cos(2.0 * np.pi * (j + 0.5) / NB)
    lags = np.arange(L)[:, None] * LSTEP
    waves = np.cos(2.0 * np.pi * (((F0 + j)[None, :] * lags) % S) / S)
    table = np.zeros((2, 8, COLS), np.float32)
    table[:, : L // 2] = (taper[None, :] * waves / np.sqrt(NB)).reshape(2, L // 2, COLS)
    return table.reshape(16, COLS)


def make_rows(rot_ref, table_ref):
    def pair(m, carry):
        turn_rows = pl.ds(pl.multiple_of(BASE + 8 * m, 8), 8)
        above = pl.multiple_of(BASE * (PAIRS + m), BASE)
        below = pl.multiple_of(BASE * (PAIRS - 1 - m), BASE)
        for v in range(FULL + 1):
            one, two = slice(256 * v, 256 * v + 128), slice(256 * v + 128, 256 * v + 256)
            turn_c = jnp.concatenate([rot_ref[turn_rows, one]] * 2, axis=0)
            turn_s = jnp.concatenate([rot_ref[turn_rows, two]] * 2, axis=0)
            for r in range(0, BASE, 16):
                c, s = rot_ref[r : r + 16, one], rot_ref[r : r + 16, two]
                cc, ss = c * turn_c, s * turn_s
                up, down = pl.ds(above + r, 16), pl.ds(below + r, 16)
                if v < FULL:
                    sc, cs = s * turn_c, c * turn_s
                    table_ref[up, one] = (cc - ss).astype(jnp.bfloat16)
                    table_ref[down, one] = (cc + ss).astype(jnp.bfloat16)
                    table_ref[up, two] = (sc + cs).astype(jnp.bfloat16)
                    table_ref[down, two] = (sc - cs).astype(jnp.bfloat16)
                else:
                    table_ref[up, one] = (cc + ss).astype(jnp.bfloat16)
                    table_ref[down, one] = (cc - ss).astype(jnp.bfloat16)
        return carry

    lax.fori_loop(0, PAIRS, pair, 0)


def lane_signs(slots, first):
    m = (lax.broadcasted_iota(jnp.int32, (slots, 128), 1) + first) % 4
    return m % 2 == 0, jnp.where(m < 2, 1.0, -1.0)


def combine(spec, slots):
    a = [spec[slots * q : slots * (q + 1), 0:128] for q in range(4)]
    b = [spec[slots * q : slots * (q + 1), 128:256] for q in range(4)]
    even, sign = lane_signs(slots, F0)
    re = jnp.where(even, a[0] + a[2] + sign * (a[1] + a[3]), a[0] - a[2] + sign * (b[1] - b[3]))
    im = jnp.where(even, b[0] + b[2] + sign * (b[1] + b[3]), b[0] - b[2] - sign * (a[1] - a[3]))
    return re, im


def combine_tail(spec, slots):
    v = [spec[slots * q : slots * (q + 1), :] for q in range(4)]
    even, sign = lane_signs(slots, F0)
    real = lax.broadcasted_iota(jnp.int32, (slots, 128), 1) < TAIL
    turned = jnp.where(real, sign, -sign) * pltpu.roll(v[1] - v[3], TAIL, 1)
    return jnp.where(even, v[0] + v[2] + sign * (v[1] + v[3]), v[0] - v[2] + turned)


def kernel(
    n,
    raw_hbm,
    index_hbm,
    count_hbm,
    rot_hbm,
    table_hbm,
    lag_hbm,
    out_ref,
    index_ref,
    count_ref,
    lag_ref,
    rot_ref,
    x_ref,
    xq_ref,
    table_ref,
    spec_ref,
    spread_ref,
    lagged_ref,
    slot_rows,
    chosen_ref,
    load_sem,
    rot_sem,
    small_sem,
    table_sem,
    far_send,
    far_recv,
    near_send,
    near_recv,
    in_send,
    in_recv,
    index_send,
    index_recv,
):
    slots = raw_hbm.shape[0]
    half = slots // 2
    me = lax.axis_index("chan")
    core = lax.axis_index("pair")
    other = 1 - core

    rot_load = pltpu.make_async_copy(rot_hbm, rot_ref, rot_sem)
    rot_load.start()
    first = pl.multiple_of(core * half, half)
    load = pltpu.make_async_copy(raw_hbm.at[pl.ds(first, half)], x_ref, load_sem)
    load.start()
    small_loads = [
        pltpu.make_async_copy(index_hbm, index_ref, small_sem.at[0]),
        pltpu.make_async_copy(count_hbm, count_ref, small_sem.at[1]),
        pltpu.make_async_copy(lag_hbm, lag_ref, small_sem.at[2]),
    ]
    table_load = pltpu.make_async_copy(table_hbm, table_ref.at[MADE:TROWS], table_sem)
    for small in small_loads:
        small.start()
    table_load.start()

    quads = n // 4
    quad, corner = me // 4, lax.rem(me, 4)
    fars = list(range(1, quads))

    def flip(value, mask):
        for bit in range(mask.bit_length()):
            if mask >> bit & 1:
                value = value + (1 << bit) - (2 << bit) * lax.rem(value // (1 << bit), 2)
        return value

    def chip(f, e):
        return 4 * flip(quad, f) + flip(corner, e)

    def around(m):
        return lax.rem(me + m, n)

    barrier = pltpu.get_barrier_semaphore()
    pl.semaphore_signal(barrier, inc=1, device_id={"pair": other})
    for m in range(1, n):
        pl.semaphore_signal(barrier, inc=1, device_id={"chan": around(m)})

    @pl.when(core == 1)
    def _():
        for f in fars:
            pl.semaphore_signal(barrier, inc=1, device_id={"chan": chip(f, 0), "pair": 0})

    rot_load.wait()
    make_rows(rot_ref, table_ref)
    table_ref[TROWS:, :] = jnp.zeros((KROWS - TROWS, COLS), jnp.bfloat16)
    load.wait()
    for q in range(4):
        rows = slice(half * q, half * (q + 1))
        xq_ref[rows, 0:QUARTER] = x_ref[:, QUARTER * q : QUARTER * (q + 1)]
        xq_ref[rows, QUARTER:] = jnp.zeros((half, KROWS - QUARTER), jnp.bfloat16)

    spectrum = jnp.dot(xq_ref[:, :MADE], table_ref[:MADE, :], preferred_element_type=jnp.float32)
    spec_ref[...] = spectrum
    table_load.wait()
    spectrum = spec_ref[...] + jnp.dot(
        xq_ref[:, MADE:], table_ref[MADE:, :], preferred_element_type=jnp.float32
    )

    parts, power = [], jnp.zeros((half, 1), jnp.float32)
    for j in range(FULL + 1):
        spec = spectrum[:, 256 * j : 256 * j + 256]
        if j < FULL:
            re, im = combine(spec, half)
            mag = re * re + im * im
            power = power + jnp.sum(mag, axis=1, keepdims=True)
        else:
            both = combine_tail(spec, half)
            square = both * both
            mag = square + pltpu.roll(square, TAIL, 1)
            power = power + jnp.sum(square, axis=1, keepdims=True)
        parts.append((re, im, mag) if j < FULL else (both, None, mag))
    floor = power * (WATER / NB) + 1e-06
    whitened = []
    for re, im, mag in parts:
        scale = lax.rsqrt(mag + floor)
        whitened.append(re * scale)
        if im is not None:
            whitened.append(im * scale)
    whitened = jnp.concatenate(whitened, axis=1).astype(jnp.bfloat16)

    spread_ref[pl.ds(pl.multiple_of(me * slots + first, half), half), :] = whitened

    def copy(block, first, rows, sends, recvs, at, device_id):
        ref = spread_ref.at[pl.ds(pl.multiple_of(block * slots + first, rows), rows), :]
        return pltpu.make_async_remote_copy(
            src_ref=ref,
            dst_ref=ref,
            send_sem=sends.at[at],
            recv_sem=recvs.at[at],
            device_id=device_id,
        )

    def far(f, i, block):
        at = 2 * f + i
        return copy(block, half * i, half, far_send, far_recv, at, {"chan": chip(f, 0), "pair": 1})

    def near(f, e, i, block):
        at = 2 * (4 * f + e) + i
        return copy(block, half * i, half, near_send, near_recv, at, {"chan": chip(0, e)})

    def inside(f, e, i):
        at = 2 * (4 * f + e) + i
        return copy(chip(f, e), half * i, half, in_send, in_recv, at, {"pair": other})

    def mates(e):
        return copy(chip(0, e), 0, slots, in_send, in_recv, 2 * e, {"pair": other})

    def index_to(m):
        return pltpu.make_async_remote_copy(
            src_ref=index_ref,
            dst_ref=slot_rows.at[me],
            send_sem=index_send.at[m],
            recv_sem=index_recv.at[m],
            device_id={"chan": around(m)},
        )

    def chosen_of(block, index):
        r_ids = lax.broadcasted_iota(jnp.int32, (slots, slots), 0)
        k_ids = lax.broadcasted_iota(jnp.int32, (slots, slots), 1)
        return jnp.where((index == r_ids) & (k_ids < count_ref[block]), 1.0, 0.0)

    def send_index():
        for small in small_loads:
            small.wait()
        for m in range(1, n):
            index_to(m).start()
        slot_rows[me] = index_ref[...]

    def choose_all():
        for m in range(1, n):
            index_to(m).wait_recv()
        none = jnp.zeros((slots, slots), jnp.bfloat16)
        for b in range(n // 2):
            left = chosen_of(2 * b, slot_rows[2 * b]).astype(jnp.bfloat16)
            right = chosen_of(2 * b + 1, slot_rows[2 * b + 1]).astype(jnp.bfloat16)
            chosen_ref[b, 0:slots, :] = jnp.concatenate([left, none], axis=1)
            chosen_ref[b, slots:, :] = jnp.concatenate([none, right], axis=1)

    def lag_rows():
        pick = chosen_of(me, index_ref[...]).T.astype(jnp.bfloat16)
        block = spread_ref[pl.ds(pl.multiple_of(me * slots, slots), slots), :]
        own = jnp.dot(pick, block, preferred_element_type=jnp.float32)
        weights = lag_ref[pl.ds(pl.multiple_of(8 * core, 8), 8), :]
        for l in range(L // 2):
            weight = weights[l : l + 1, :]
            lagged_ref[slots * l : slots * (l + 1), :] = (own * weight).astype(jnp.bfloat16)

    def correlate(f, e):
        at = pl.multiple_of(chip(f, e) // 2 * 2 * slots, 2 * slots)
        product = lax.dot_general(
            lagged_ref[...],
            spread_ref[pl.ds(at, 2 * slots), :],
            (((1,), (1,)), ((), ())),
            preferred_element_type=jnp.float32,
        ).astype(jnp.bfloat16)
        product = jnp.dot(
            product, chosen_ref[chip(f, e) // 2], preferred_element_type=jnp.float32
        ).astype(jnp.bfloat16)
        for l in range(L // 2):
            out_ref[l, :, pl.ds(at, 2 * slots)] = product[slots * l : slots * (l + 1)]

    @pl.when(core == 0)
    def _():
        pl.semaphore_wait(barrier, n + quads - 1)
        for f in fars:
            far(f, 0, me).start()
        for e in (1, 3, 2):
            near(0, e, 0, me).start()
        inside(0, 0, 0).start()
        send_index()
        inside(0, 0, 1).wait_recv()
        for e in (1, 3, 2):
            near(0, e, 1, me).start()
        lag_rows()
        choose_all()
        for e in (1, 3, 2):
            for i in (0, 1):
                near(0, e, i, me).wait_recv()
            mates(e).start()
        correlate(0, 0)
        correlate(0, 2)
        for f in fars:
            for pair in ((0, 1), (2, 3)):
                for e in pair:
                    for i in (1, 0):
                        inside(f, e, i).wait_recv()
                correlate(f, pair[0])
        inside(0, 0, 0).wait_send()
        for f in fars:
            far(f, 0, me).wait_send()
        for e in (1, 3, 2):
            for i in (0, 1):
                near(0, e, i, me).wait_send()
            mates(e).wait_send()
        for m in range(1, n):
            index_to(m).wait_send()

    @pl.when(core == 1)
    def _():
        pl.semaphore_wait(barrier, n)
        for f in fars:
            far(f, 1, me).start()
        inside(0, 0, 1).start()
        send_index()
        for f in fars:
            for i in (1, 0):
                far(f, i, me).wait_recv()
                for e in (3, 2, 1):
                    near(f, e, i, chip(f, 0)).start()
                inside(f, 0, i).start()
        inside(0, 0, 0).wait_recv()
        lag_rows()
        choose_all()
        for f in fars:
            for i in (1, 0):
                for e in (1, 2, 3):
                    near(f, e, i, me).wait_recv()
                    inside(f, e, i).start()
            correlate(f, 0)
            correlate(f, 2)
        for e in (1, 3, 2):
            mates(e).wait_recv()
        correlate(0, 0)
        correlate(0, 2)
        inside(0, 0, 1).wait_send()
        for f in fars:
            far(f, 1, me).wait_send()
            for i in (1, 0):
                for e in (1, 2, 3):
                    near(f, e, i, me).wait_send()
                    inside(f, e, i).wait_send()
                inside(f, 0, i).wait_send()
        for m in range(1, n):
            index_to(m).wait_send()


def shards(n, raw, live_index, live_count):
    slots = raw.shape[0]
    vmem = pl.BlockSpec(memory_space=pltpu.VMEM)
    return pl.pallas_call(
        functools.partial(kernel, n),
        out_shape=pltpu.VMEM((L // 2, slots, n * slots), jnp.bfloat16),
        in_specs=[
            pl.BlockSpec(memory_space=pl.ANY),
            pl.BlockSpec(memory_space=pl.ANY),
            pl.BlockSpec(memory_space=pl.ANY),
            pl.BlockSpec(memory_space=pl.ANY),
            pl.BlockSpec(memory_space=pl.ANY),
            pl.BlockSpec(memory_space=pl.ANY),
        ],
        out_specs=vmem,
        scratch_shapes=[
            pltpu.VMEM((1, slots), jnp.int32),
            pltpu.SMEM((n,), jnp.int32),
            pltpu.VMEM((16, COLS), jnp.float32),
            pltpu.VMEM((BASE + 8 * PAIRS, COLS + 128), jnp.float32),
            pltpu.VMEM((slots // 2, S), jnp.bfloat16),
            pltpu.VMEM((2 * slots, KROWS), jnp.bfloat16),
            pltpu.VMEM((KROWS, COLS), jnp.bfloat16),
            pltpu.VMEM((2 * slots, COLS), jnp.float32),
            pltpu.VMEM((n * slots, COLS), jnp.bfloat16),
            pltpu.VMEM((L // 2 * slots, COLS), jnp.bfloat16),
            pltpu.VMEM((n, 1, slots), jnp.int32),
            pltpu.VMEM((n // 2, 2 * slots, 2 * slots), jnp.bfloat16),
            pltpu.SemaphoreType.DMA,
            pltpu.SemaphoreType.DMA,
            pltpu.SemaphoreType.DMA((3,)),
            pltpu.SemaphoreType.DMA,
            pltpu.SemaphoreType.DMA((n // 2,)),
            pltpu.SemaphoreType.DMA((n // 2,)),
            pltpu.SemaphoreType.DMA((2 * n,)),
            pltpu.SemaphoreType.DMA((2 * n,)),
            pltpu.SemaphoreType.DMA((2 * n,)),
            pltpu.SemaphoreType.DMA((2 * n,)),
            pltpu.SemaphoreType.DMA((n,)),
            pltpu.SemaphoreType.DMA((n,)),
        ],
        compiler_params=pltpu.CompilerParams(
            collective_id=0, has_side_effects=True, vmem_limit_bytes=VMEM_LIMIT - 6 * slots * n * slots
        ),
    )(
        raw.reshape(slots, S),
        live_index,
        live_count,
        jnp.asarray(rotation_table()),
        jnp.asarray(dft_table(), jnp.bfloat16),
        jnp.asarray(lag_table()),
    )


def solution(mesh):
    return jax.shard_map(
        functools.partial(shards, mesh.shape["chan"]),
        mesh=mesh,
        in_specs=(P(("groups", "chan"), None, None), P(("groups", "chan"), None), P("groups")),
        out_specs=P("pair", ("groups", "chan"), None),
        check_vma=False,
    )
```

```python
import functools

import jax
import jax.numpy as jnp
import numpy as np
from jax import lax
from jax.experimental import pallas as pl
from jax.experimental.pallas import tpu as pltpu
from jax.sharding import PartitionSpec as P

S = 12000
NB = 448
L = 6
LSTEP = 125
F0 = 60
WATER = 0.1
QUARTER = S // 4
BASE = 128
BASE_STEP = 32
PAIRS = 7
MADE = 2 * BASE * PAIRS
KROWS = 3072
TROWS = 3008
FULL = NB // 128
TAIL = NB - 128 * FULL
COLS = 2 * NB
VMEM_LIMIT = 63_300_000


def column_bins():
    full = np.arange(128 * FULL).reshape(FULL, 1, 128)
    tail = np.arange(128 * FULL, NB)
    return np.concatenate([np.repeat(full, 2, axis=1).reshape(-1), tail, tail])


def column_is_sine():
    full = np.repeat(np.arange(2) == 1, 128)
    return np.concatenate([np.tile(full, FULL), np.repeat(np.arange(2) == 1, TAIL)])


def dft_table():
    phase = np.arange(MADE, QUARTER)[:, None] * (F0 + column_bins())[None, :] % S
    angle = (phase.astype(np.float32) * np.float32(2.0 * np.pi / S)).astype(np.float64)
    out = np.zeros((TROWS - MADE, COLS), np.float32)
    out[: QUARTER - MADE] = np.where(column_is_sine()[None, :], -np.sin(angle), np.cos(angle))
    return out


def lag_table():
    j = column_bins()
    taper = 0.5 - 0.5 * np.cos(2.0 * np.pi * (j + 0.5) / NB)
    lags = np.arange(L)[:, None] * LSTEP
    waves = np.cos(2.0 * np.pi * (((F0 + j)[None, :] * lags) % S) / S)
    table = np.zeros((2, 8, COLS), np.float32)
    table[:, : L // 2] = (taper[None, :] * waves / np.sqrt(NB)).reshape(2, L // 2, COLS)
    return table.reshape(16, COLS)


def cosine_and_minus_sine(step, bins, shift=0.0):
    phase = step * (bins + F0)
    turns = jnp.floor(phase * (4.0 / S) + 0.5)
    x = (phase - turns * (S / 4)) * (2.0 * np.pi / S) + shift
    y = x * x
    c = 1.0 + y * (-0.5 + y * (1 / 24 + y * (-1 / 720 + y * (1 / 40320))))
    s = -x * (1.0 + y * (-1 / 6 + y * (1 / 120 + y * (-1 / 5040 + y * (1 / 362880)))))
    turns = turns - 4.0 * jnp.floor(turns * 0.25)
    odd = (turns == 1.0) | (turns == 3.0)
    cosine, minus_sine = jnp.where(odd, s, c), jnp.where(odd, -c, s)
    back = turns >= 2.0
    return jnp.where(back, -cosine, cosine), jnp.where(back, -minus_sine, minus_sine)


def lane_bins(rows, v):
    lane = lax.broadcasted_iota(jnp.int32, (rows, 128), 1)
    if v == FULL:
        lane = jnp.where(lane < TAIL, lane, lane - TAIL)
    return (lane + 128 * v).astype(jnp.float32)


def make_base(rot_ref):
    unit = 2.0 * np.pi / S
    shift = np.pi * (float(np.float32(unit)) / unit - 1.0)
    cosine = lax.broadcasted_iota(jnp.int32, (BASE_STEP, 128), 1) < TAIL

    def rows_of(i, carry):
        at = pl.ds(pl.multiple_of(i * BASE_STEP, BASE_STEP), BASE_STEP)
        row = lax.broadcasted_iota(jnp.int32, (BASE_STEP, 128), 0) + i * BASE_STEP
        step = (row + (BASE * PAIRS - BASE // 2)).astype(jnp.float32)
        for v in range(FULL + 1):
            c, s = cosine_and_minus_sine(step, lane_bins(BASE_STEP, v), shift)
            if v == FULL:
                c, s = jnp.where(cosine, c, s), jnp.where(cosine, s, c)
            rot_ref[at, 256 * v : 256 * v + 128] = c
            rot_ref[at, 256 * v + 128 : 256 * v + 256] = s
        return carry

    lax.fori_loop(0, BASE // BASE_STEP, rows_of, 0)


def make_rows(rot_ref, table_ref):
    cosine = lax.broadcasted_iota(jnp.int32, (8, 128), 1) < TAIL

    def pair(m, carry):
        step = (jnp.full((8, 128), BASE // 2, jnp.int32) * (2 * m + 1)).astype(jnp.float32)
        above = pl.multiple_of(BASE * (PAIRS + m), BASE)
        below = pl.multiple_of(BASE * (PAIRS - 1 - m), BASE)
        for v in range(FULL + 1):
            one, two = slice(256 * v, 256 * v + 128), slice(256 * v + 128, 256 * v + 256)
            turn_c, turn_s = cosine_and_minus_sine(step, lane_bins(8, v))
            if v == FULL:
                turn_s = jnp.where(cosine, -turn_s, turn_s)
            turn_c = jnp.concatenate([turn_c] * 2, axis=0)
            turn_s = jnp.concatenate([turn_s] * 2, axis=0)
            for r in range(0, BASE, 16):
                c, s = rot_ref[r : r + 16, one], rot_ref[r : r + 16, two]
                cc, ss = c * turn_c, s * turn_s
                up, down = pl.ds(above + r, 16), pl.ds(below + r, 16)
                if v < FULL:
                    sc, cs = s * turn_c, c * turn_s
                    table_ref[up, one] = (cc - ss).astype(jnp.bfloat16)
                    table_ref[down, one] = (cc + ss).astype(jnp.bfloat16)
                    table_ref[up, two] = (sc + cs).astype(jnp.bfloat16)
                    table_ref[down, two] = (sc - cs).astype(jnp.bfloat16)
                else:
                    table_ref[up, one] = (cc + ss).astype(jnp.bfloat16)
                    table_ref[down, one] = (cc - ss).astype(jnp.bfloat16)
        return carry

    lax.fori_loop(0, PAIRS, pair, 0)


def lane_signs(slots, first):
    m = (lax.broadcasted_iota(jnp.int32, (slots, 128), 1) + first) % 4
    return m % 2 == 0, jnp.where(m < 2, 1.0, -1.0)


def combine(spec, slots):
    a = [spec[slots * q : slots * (q + 1), 0:128] for q in range(4)]
    b = [spec[slots * q : slots * (q + 1), 128:256] for q in range(4)]
    even, sign = lane_signs(slots, F0)
    re = jnp.where(even, a[0] + a[2] + sign * (a[1] + a[3]), a[0] - a[2] + sign * (b[1] - b[3]))
    im = jnp.where(even, b[0] + b[2] + sign * (b[1] + b[3]), b[0] - b[2] - sign * (a[1] - a[3]))
    return re, im


def combine_tail(spec, slots):
    v = [spec[slots * q : slots * (q + 1), :] for q in range(4)]
    even, sign = lane_signs(slots, F0)
    real = lax.broadcasted_iota(jnp.int32, (slots, 128), 1) < TAIL
    turned = jnp.where(real, sign, -sign) * pltpu.roll(v[1] - v[3], TAIL, 1)
    return jnp.where(even, v[0] + v[2] + sign * (v[1] + v[3]), v[0] - v[2] + turned)


def kernel(
    n,
    raw_hbm,
    index_hbm,
    count_hbm,
    table_hbm,
    lag_hbm,
    out_ref,
    index_ref,
    count_ref,
    lag_ref,
    rot_ref,
    x_ref,
    xq_ref,
    table_ref,
    spec_ref,
    spread_ref,
    lagged_ref,
    slot_rows,
    chosen_ref,
    load_sem,
    small_sem,
    table_sem,
    far_send,
    far_recv,
    near_send,
    near_recv,
    in_send,
    in_recv,
    index_send,
    index_recv,
):
    slots = raw_hbm.shape[0]
    half = slots // 2
    me = lax.axis_index("chan")
    core = lax.axis_index("pair")
    other = 1 - core

    first = pl.multiple_of(core * half, half)
    load = pltpu.make_async_copy(raw_hbm.at[pl.ds(first, half)], x_ref, load_sem)
    load.start()
    small_loads = [
        pltpu.make_async_copy(index_hbm, index_ref, small_sem.at[0]),
        pltpu.make_async_copy(count_hbm, count_ref, small_sem.at[1]),
        pltpu.make_async_copy(lag_hbm, lag_ref, small_sem.at[2]),
    ]
    table_load = pltpu.make_async_copy(table_hbm, table_ref.at[MADE:TROWS], table_sem)
    for small in small_loads:
        small.start()
    table_load.start()

    quads = n // 4
    quad, corner = me // 4, lax.rem(me, 4)
    fars = list(range(1, quads))

    def flip(value, mask):
        for bit in range(mask.bit_length()):
            if mask >> bit & 1:
                value = value + (1 << bit) - (2 << bit) * lax.rem(value // (1 << bit), 2)
        return value

    def chip(f, e):
        return 4 * flip(quad, f) + flip(corner, e)

    def around(m):
        return lax.rem(me + m, n)

    barrier = pltpu.get_barrier_semaphore()
    pl.semaphore_signal(barrier, inc=1, device_id={"pair": other})
    for m in range(1, n):
        pl.semaphore_signal(barrier, inc=1, device_id={"chan": around(m)})

    @pl.when(core == 1)
    def _():
        for f in fars:
            pl.semaphore_signal(barrier, inc=1, device_id={"chan": chip(f, 0), "pair": 0})

    make_base(rot_ref)
    make_rows(rot_ref, table_ref)
    table_ref[TROWS:, :] = jnp.zeros((KROWS - TROWS, COLS), jnp.bfloat16)
    load.wait()
    for q in range(4):
        rows = slice(half * q, half * (q + 1))
        xq_ref[rows, 0:QUARTER] = x_ref[:, QUARTER * q : QUARTER * (q + 1)]
        xq_ref[rows, QUARTER:] = jnp.zeros((half, KROWS - QUARTER), jnp.bfloat16)

    spectrum = jnp.dot(xq_ref[:, :MADE], table_ref[:MADE, :], preferred_element_type=jnp.float32)
    spec_ref[...] = spectrum
    table_load.wait()
    spectrum = spec_ref[...] + jnp.dot(
        xq_ref[:, MADE:], table_ref[MADE:, :], preferred_element_type=jnp.float32
    )

    parts, power = [], jnp.zeros((half, 1), jnp.float32)
    for j in range(FULL + 1):
        spec = spectrum[:, 256 * j : 256 * j + 256]
        if j < FULL:
            re, im = combine(spec, half)
            mag = re * re + im * im
            power = power + jnp.sum(mag, axis=1, keepdims=True)
        else:
            both = combine_tail(spec, half)
            square = both * both
            mag = square + pltpu.roll(square, TAIL, 1)
            power = power + jnp.sum(square, axis=1, keepdims=True)
        parts.append((re, im, mag) if j < FULL else (both, None, mag))
    floor = power * (WATER / NB) + 1e-06
    whitened = []
    for re, im, mag in parts:
        scale = lax.rsqrt(mag + floor)
        whitened.append(re * scale)
        if im is not None:
            whitened.append(im * scale)
    whitened = jnp.concatenate(whitened, axis=1).astype(jnp.bfloat16)

    spread_ref[pl.ds(pl.multiple_of(me * slots + first, half), half), :] = whitened

    def copy(block, first, rows, sends, recvs, at, device_id):
        ref = spread_ref.at[pl.ds(pl.multiple_of(block * slots + first, rows), rows), :]
        return pltpu.make_async_remote_copy(
            src_ref=ref,
            dst_ref=ref,
            send_sem=sends.at[at],
            recv_sem=recvs.at[at],
            device_id=device_id,
        )

    def far(f, i, block):
        at = 2 * f + i
        return copy(block, half * i, half, far_send, far_recv, at, {"chan": chip(f, 0), "pair": 1})

    def near(f, e, i, block):
        at = 2 * (4 * f + e) + i
        return copy(block, half * i, half, near_send, near_recv, at, {"chan": chip(0, e)})

    def inside(f, e, i):
        at = 2 * (4 * f + e) + i
        return copy(chip(f, e), half * i, half, in_send, in_recv, at, {"pair": other})

    def mates(e):
        return copy(chip(0, e), 0, slots, in_send, in_recv, 2 * e, {"pair": other})

    def index_to(m):
        return pltpu.make_async_remote_copy(
            src_ref=index_ref,
            dst_ref=slot_rows.at[me],
            send_sem=index_send.at[m],
            recv_sem=index_recv.at[m],
            device_id={"chan": around(m)},
        )

    def chosen_of(block, index):
        r_ids = lax.broadcasted_iota(jnp.int32, (slots, slots), 0)
        k_ids = lax.broadcasted_iota(jnp.int32, (slots, slots), 1)
        return jnp.where((index == r_ids) & (k_ids < count_ref[block]), 1.0, 0.0)

    def send_index():
        for small in small_loads:
            small.wait()
        for m in range(1, n):
            index_to(m).start()
        slot_rows[me] = index_ref[...]

    def choose_all():
        for m in range(1, n):
            index_to(m).wait_recv()
        none = jnp.zeros((slots, slots), jnp.bfloat16)
        for b in range(n // 2):
            left = chosen_of(2 * b, slot_rows[2 * b]).astype(jnp.bfloat16)
            right = chosen_of(2 * b + 1, slot_rows[2 * b + 1]).astype(jnp.bfloat16)
            chosen_ref[b, 0:slots, :] = jnp.concatenate([left, none], axis=1)
            chosen_ref[b, slots:, :] = jnp.concatenate([none, right], axis=1)

    def lag_rows():
        pick = chosen_of(me, index_ref[...]).T.astype(jnp.bfloat16)
        block = spread_ref[pl.ds(pl.multiple_of(me * slots, slots), slots), :]
        own = jnp.dot(pick, block, preferred_element_type=jnp.float32)
        weights = lag_ref[pl.ds(pl.multiple_of(8 * core, 8), 8), :]
        for l in range(L // 2):
            weight = weights[l : l + 1, :]
            lagged_ref[slots * l : slots * (l + 1), :] = (own * weight).astype(jnp.bfloat16)

    def correlate(f, e):
        at = pl.multiple_of(chip(f, e) // 2 * 2 * slots, 2 * slots)
        product = lax.dot_general(
            lagged_ref[...],
            spread_ref[pl.ds(at, 2 * slots), :],
            (((1,), (1,)), ((), ())),
            preferred_element_type=jnp.float32,
        ).astype(jnp.bfloat16)
        product = jnp.dot(
            product, chosen_ref[chip(f, e) // 2], preferred_element_type=jnp.float32
        ).astype(jnp.bfloat16)
        for l in range(L // 2):
            out_ref[l, :, pl.ds(at, 2 * slots)] = product[slots * l : slots * (l + 1)]

    @pl.when(core == 0)
    def _():
        pl.semaphore_wait(barrier, n + quads - 1)
        for f in fars:
            far(f, 0, me).start()
        for e in (1, 3, 2):
            near(0, e, 0, me).start()
        inside(0, 0, 0).start()
        send_index()
        inside(0, 0, 1).wait_recv()
        for e in (1, 3, 2):
            near(0, e, 1, me).start()
        lag_rows()
        choose_all()
        for e in (1, 3, 2):
            for i in (0, 1):
                near(0, e, i, me).wait_recv()
            mates(e).start()
        correlate(0, 0)
        correlate(0, 2)
        for f in fars:
            for pair in ((0, 1), (2, 3)):
                for e in pair:
                    for i in (1, 0):
                        inside(f, e, i).wait_recv()
                correlate(f, pair[0])
        inside(0, 0, 0).wait_send()
        for f in fars:
            far(f, 0, me).wait_send()
        for e in (1, 3, 2):
            for i in (0, 1):
                near(0, e, i, me).wait_send()
            mates(e).wait_send()
        for m in range(1, n):
            index_to(m).wait_send()

    @pl.when(core == 1)
    def _():
        pl.semaphore_wait(barrier, n)
        for f in fars:
            far(f, 1, me).start()
        inside(0, 0, 1).start()
        send_index()
        for f in fars:
            for i in (1, 0):
                far(f, i, me).wait_recv()
                for e in (3, 2, 1):
                    near(f, e, i, chip(f, 0)).start()
                inside(f, 0, i).start()
        inside(0, 0, 0).wait_recv()
        lag_rows()
        choose_all()
        for f in fars:
            for i in (1, 0):
                for e in (1, 2, 3):
                    near(f, e, i, me).wait_recv()
                    inside(f, e, i).start()
            correlate(f, 0)
            correlate(f, 2)
        for e in (1, 3, 2):
            mates(e).wait_recv()
        correlate(0, 0)
        correlate(0, 2)
        inside(0, 0, 1).wait_send()
        for f in fars:
            far(f, 1, me).wait_send()
            for i in (1, 0):
                for e in (1, 2, 3):
                    near(f, e, i, me).wait_send()
                    inside(f, e, i).wait_send()
                inside(f, 0, i).wait_send()
        for m in range(1, n):
            index_to(m).wait_send()


def shards(n, raw, live_index, live_count):
    slots = raw.shape[0]
    vmem = pl.BlockSpec(memory_space=pltpu.VMEM)
    return pl.pallas_call(
        functools.partial(kernel, n),
        out_shape=pltpu.VMEM((L // 2, slots, n * slots), jnp.bfloat16),
        in_specs=[
            pl.BlockSpec(memory_space=pl.ANY),
            pl.BlockSpec(memory_space=pl.ANY),
            pl.BlockSpec(memory_space=pl.ANY),
            pl.BlockSpec(memory_space=pl.ANY),
            pl.BlockSpec(memory_space=pl.ANY),
        ],
        out_specs=vmem,
        scratch_shapes=[
            pltpu.VMEM((1, slots), jnp.int32),
            pltpu.SMEM((n,), jnp.int32),
            pltpu.VMEM((16, COLS), jnp.float32),
            pltpu.VMEM((BASE, COLS + 128), jnp.float32),
            pltpu.VMEM((slots // 2, S), jnp.bfloat16),
            pltpu.VMEM((2 * slots, KROWS), jnp.bfloat16),
            pltpu.VMEM((KROWS, COLS), jnp.bfloat16),
            pltpu.VMEM((2 * slots, COLS), jnp.float32),
            pltpu.VMEM((n * slots, COLS), jnp.bfloat16),
            pltpu.VMEM((L // 2 * slots, COLS), jnp.bfloat16),
            pltpu.VMEM((n, 1, slots), jnp.int32),
            pltpu.VMEM((n // 2, 2 * slots, 2 * slots), jnp.bfloat16),
            pltpu.SemaphoreType.DMA,
            pltpu.SemaphoreType.DMA((3,)),
            pltpu.SemaphoreType.DMA,
            pltpu.SemaphoreType.DMA((n // 2,)),
            pltpu.SemaphoreType.DMA((n // 2,)),
            pltpu.SemaphoreType.DMA((2 * n,)),
            pltpu.SemaphoreType.DMA((2 * n,)),
            pltpu.SemaphoreType.DMA((2 * n,)),
            pltpu.SemaphoreType.DMA((2 * n,)),
            pltpu.SemaphoreType.DMA((n,)),
            pltpu.SemaphoreType.DMA((n,)),
        ],
        compiler_params=pltpu.CompilerParams(
            collective_id=0, has_side_effects=True, vmem_limit_bytes=VMEM_LIMIT - 6 * slots * n * slots
        ),
    )(
        raw.reshape(slots, S),
        live_index,
        live_count,
        jnp.asarray(dft_table(), jnp.bfloat16),
        jnp.asarray(lag_table()),
    )


def solution(mesh):
    return jax.shard_map(
        functools.partial(shards, mesh.shape["chan"]),
        mesh=mesh,
        in_specs=(P(("groups", "chan"), None, None), P(("groups", "chan"), None), P("groups")),
        out_specs=P("pair", ("groups", "chan"), None),
        check_vma=False,
    )
```

```python
import functools

import jax
import jax.numpy as jnp
import numpy as np
from jax import lax
from jax.experimental import pallas as pl
from jax.experimental.pallas import tpu as pltpu
from jax.sharding import PartitionSpec as P

S = 12000
NB = 448
L = 6
LSTEP = 125
F0 = 60
WATER = 0.1
QUARTER = S // 4
BASE = 128
BASE_STEP = 32
PAIRS = 7
MADE = 2 * BASE * PAIRS
KROWS = 3072
TROWS = 3008
FULL = NB // 128
TAIL = NB - 128 * FULL
COLS = 2 * NB
VMEM_LIMIT = 63_300_000


def column_bins():
    full = np.arange(128 * FULL).reshape(FULL, 1, 128)
    tail = np.arange(128 * FULL, NB)
    return np.concatenate([np.repeat(full, 2, axis=1).reshape(-1), tail, tail])


def column_is_sine():
    full = np.repeat(np.arange(2) == 1, 128)
    return np.concatenate([np.tile(full, FULL), np.repeat(np.arange(2) == 1, TAIL)])


def dft_table():
    phase = np.arange(MADE, QUARTER)[:, None] * (F0 + column_bins())[None, :] % S
    angle = (phase.astype(np.float32) * np.float32(2.0 * np.pi / S)).astype(np.float64)
    out = np.zeros((TROWS - MADE, COLS), np.float32)
    out[: QUARTER - MADE] = np.where(column_is_sine()[None, :], -np.sin(angle), np.cos(angle))
    return out


def lag_table():
    j = column_bins()
    taper = 0.5 - 0.5 * np.cos(2.0 * np.pi * (j + 0.5) / NB)
    lags = np.arange(L)[:, None] * LSTEP
    waves = np.cos(2.0 * np.pi * (((F0 + j)[None, :] * lags) % S) / S)
    table = np.zeros((2, 8, COLS), np.float32)
    table[:, : L // 2] = (taper[None, :] * waves / np.sqrt(NB)).reshape(2, L // 2, COLS)
    return table.reshape(16, COLS)


def cosine_and_minus_sine(step, bins, shift=0.0):
    phase = step * (bins + F0)
    turns = jnp.floor(phase * (4.0 / S) + 0.5)
    x = (phase - turns * (S / 4)) * (2.0 * np.pi / S) + shift
    y = x * x
    c = 1.0 + y * (-0.5 + y * (1 / 24 + y * (-1 / 720 + y * (1 / 40320))))
    s = -x * (1.0 + y * (-1 / 6 + y * (1 / 120 + y * (-1 / 5040 + y * (1 / 362880)))))
    turns = turns - 4.0 * jnp.floor(turns * 0.25)
    odd = (turns == 1.0) | (turns == 3.0)
    cosine, minus_sine = jnp.where(odd, s, c), jnp.where(odd, -c, s)
    back = turns >= 2.0
    return jnp.where(back, -cosine, cosine), jnp.where(back, -minus_sine, minus_sine)


def lane_bins(rows, v):
    lane = lax.broadcasted_iota(jnp.int32, (rows, 128), 1)
    if v == FULL:
        lane = jnp.where(lane < TAIL, lane, lane - TAIL)
    return (lane + 128 * v).astype(jnp.float32)


def make_base(rot_ref):
    unit = 2.0 * np.pi / S
    shift = np.pi * (float(np.float32(unit)) / unit - 1.0)
    cosine = lax.broadcasted_iota(jnp.int32, (BASE_STEP, 128), 1) < TAIL

    def rows_of(i, carry):
        at = pl.ds(pl.multiple_of(i * BASE_STEP, BASE_STEP), BASE_STEP)
        row = lax.broadcasted_iota(jnp.int32, (BASE_STEP, 128), 0) + i * BASE_STEP
        step = (row + (BASE * PAIRS - BASE // 2)).astype(jnp.float32)
        for v in range(FULL + 1):
            c, s = cosine_and_minus_sine(step, lane_bins(BASE_STEP, v), shift)
            if v == FULL:
                c, s = jnp.where(cosine, c, s), jnp.where(cosine, s, c)
            rot_ref[at, 256 * v : 256 * v + 128] = c
            rot_ref[at, 256 * v + 128 : 256 * v + 256] = s
        return carry

    lax.fori_loop(0, BASE // BASE_STEP, rows_of, 0)


def make_rows(rot_ref, table_ref):
    cosine = lax.broadcasted_iota(jnp.int32, (8, 128), 1) < TAIL

    def pair(m, carry):
        step = (jnp.full((8, 128), BASE // 2, jnp.int32) * (2 * m + 1)).astype(jnp.float32)
        above = pl.multiple_of(BASE * (PAIRS + m), BASE)
        below = pl.multiple_of(BASE * (PAIRS - 1 - m), BASE)
        for v in range(FULL + 1):
            one, two = slice(256 * v, 256 * v + 128), slice(256 * v + 128, 256 * v + 256)
            turn_c, turn_s = cosine_and_minus_sine(step, lane_bins(8, v))
            if v == FULL:
                turn_s = jnp.where(cosine, -turn_s, turn_s)
            turn_c = jnp.concatenate([turn_c] * 2, axis=0)
            turn_s = jnp.concatenate([turn_s] * 2, axis=0)
            for r in range(0, BASE, 16):
                c, s = rot_ref[r : r + 16, one], rot_ref[r : r + 16, two]
                cc, ss = c * turn_c, s * turn_s
                up, down = pl.ds(above + r, 16), pl.ds(below + r, 16)
                if v < FULL:
                    sc, cs = s * turn_c, c * turn_s
                    table_ref[up, one] = (cc - ss).astype(jnp.bfloat16)
                    table_ref[down, one] = (cc + ss).astype(jnp.bfloat16)
                    table_ref[up, two] = (sc + cs).astype(jnp.bfloat16)
                    table_ref[down, two] = (sc - cs).astype(jnp.bfloat16)
                else:
                    table_ref[up, one] = (cc + ss).astype(jnp.bfloat16)
                    table_ref[down, one] = (cc - ss).astype(jnp.bfloat16)
        return carry

    lax.fori_loop(0, PAIRS, pair, 0)


def lane_signs(slots, first):
    m = (lax.broadcasted_iota(jnp.int32, (slots, 128), 1) + first) % 4
    return m % 2 == 0, jnp.where(m < 2, 1.0, -1.0)


def combine(spec, slots):
    a = [spec[slots * q : slots * (q + 1), 0:128] for q in range(4)]
    b = [spec[slots * q : slots * (q + 1), 128:256] for q in range(4)]
    even, sign = lane_signs(slots, F0)
    re = jnp.where(even, a[0] + a[2] + sign * (a[1] + a[3]), a[0] - a[2] + sign * (b[1] - b[3]))
    im = jnp.where(even, b[0] + b[2] + sign * (b[1] + b[3]), b[0] - b[2] - sign * (a[1] - a[3]))
    return re, im


def combine_tail(spec, slots):
    v = [spec[slots * q : slots * (q + 1), :] for q in range(4)]
    even, sign = lane_signs(slots, F0)
    real = lax.broadcasted_iota(jnp.int32, (slots, 128), 1) < TAIL
    turned = jnp.where(real, sign, -sign) * pltpu.roll(v[1] - v[3], TAIL, 1)
    return jnp.where(even, v[0] + v[2] + sign * (v[1] + v[3]), v[0] - v[2] + turned)


def kernel(
    n,
    raw_hbm,
    index_hbm,
    count_hbm,
    table_hbm,
    lag_hbm,
    out_ref,
    index_ref,
    count_ref,
    lag_ref,
    rot_ref,
    x_ref,
    xq_ref,
    table_ref,
    spec_ref,
    spread_ref,
    lagged_ref,
    slot_rows,
    chosen_ref,
    load_sem,
    small_sem,
    table_sem,
    far_send,
    far_recv,
    near_send,
    near_recv,
    in_send,
    in_recv,
    index_send,
    index_recv,
):
    slots = raw_hbm.shape[0]
    half = slots // 2
    me = lax.axis_index("chan")
    core = lax.axis_index("pair")
    other = 1 - core

    first = pl.multiple_of(core * half, half)
    load = pltpu.make_async_copy(raw_hbm.at[pl.ds(first, half)], x_ref, load_sem)
    load.start()
    small_loads = [
        pltpu.make_async_copy(index_hbm, index_ref, small_sem.at[0]),
        pltpu.make_async_copy(count_hbm, count_ref, small_sem.at[1]),
        pltpu.make_async_copy(lag_hbm, lag_ref, small_sem.at[2]),
    ]
    table_load = pltpu.make_async_copy(table_hbm, table_ref.at[MADE:TROWS], table_sem)
    for small in small_loads:
        small.start()
    table_load.start()

    quads = n // 4
    quad, corner = me // 4, lax.rem(me, 4)
    fars = list(range(1, quads))

    def flip(value, mask):
        for bit in range(mask.bit_length()):
            if mask >> bit & 1:
                value = value + (1 << bit) - (2 << bit) * lax.rem(value // (1 << bit), 2)
        return value

    def chip(f, e):
        return 4 * flip(quad, f) + flip(corner, e)

    def around(m):
        return lax.rem(me + m, n)

    barrier = pltpu.get_barrier_semaphore()
    pl.semaphore_signal(barrier, inc=1, device_id={"pair": other})
    for e in (1, 2, 3):
        pl.semaphore_signal(barrier, inc=1, device_id={"chan": chip(0, e)})

    @pl.when(core == 0)
    def _():
        for e in (1, 2, 3):
            pl.semaphore_signal(barrier, inc=1, device_id={"chan": chip(0, e), "pair": 1})

    @pl.when(core == 1)
    def _():
        for m in range(1, n):
            pl.semaphore_signal(barrier, inc=1, device_id={"chan": around(m)})
        for f in fars:
            pl.semaphore_signal(barrier, inc=1, device_id={"chan": chip(f, 0), "pair": 0})

    make_base(rot_ref)
    make_rows(rot_ref, table_ref)
    table_ref[TROWS:, :] = jnp.zeros((KROWS - TROWS, COLS), jnp.bfloat16)
    load.wait()
    for q in range(4):
        rows = slice(half * q, half * (q + 1))
        xq_ref[rows, 0:QUARTER] = x_ref[:, QUARTER * q : QUARTER * (q + 1)]
        xq_ref[rows, QUARTER:] = jnp.zeros((half, KROWS - QUARTER), jnp.bfloat16)

    spectrum = jnp.dot(xq_ref[:, :MADE], table_ref[:MADE, :], preferred_element_type=jnp.float32)
    spec_ref[...] = spectrum
    table_load.wait()
    spectrum = spec_ref[...] + jnp.dot(
        xq_ref[:, MADE:], table_ref[MADE:, :], preferred_element_type=jnp.float32
    )

    parts, power = [], jnp.zeros((half, 1), jnp.float32)
    for j in range(FULL + 1):
        spec = spectrum[:, 256 * j : 256 * j + 256]
        if j < FULL:
            re, im = combine(spec, half)
            mag = re * re + im * im
            power = power + jnp.sum(mag, axis=1, keepdims=True)
        else:
            both = combine_tail(spec, half)
            square = both * both
            mag = square + pltpu.roll(square, TAIL, 1)
            power = power + jnp.sum(square, axis=1, keepdims=True)
        parts.append((re, im, mag) if j < FULL else (both, None, mag))
    floor = power * (WATER / NB) + 1e-06
    whitened = []
    for re, im, mag in parts:
        scale = lax.rsqrt(mag + floor)
        whitened.append(re * scale)
        if im is not None:
            whitened.append(im * scale)
    whitened = jnp.concatenate(whitened, axis=1).astype(jnp.bfloat16)

    spread_ref[pl.ds(pl.multiple_of(me * slots + first, half), half), :] = whitened

    def copy(block, first, rows, sends, recvs, at, device_id):
        ref = spread_ref.at[pl.ds(pl.multiple_of(block * slots + first, rows), rows), :]
        return pltpu.make_async_remote_copy(
            src_ref=ref,
            dst_ref=ref,
            send_sem=sends.at[at],
            recv_sem=recvs.at[at],
            device_id=device_id,
        )

    def far(f, i, block):
        at = 2 * f + i
        return copy(block, half * i, half, far_send, far_recv, at, {"chan": chip(f, 0), "pair": 1})

    def near(f, e, i, block):
        at = 2 * (4 * f + e) + i
        return copy(block, half * i, half, near_send, near_recv, at, {"chan": chip(0, e)})

    def mine(e, i):
        at = 2 * e + i
        return copy(me, half * i, half, near_send, near_recv, at, {"chan": chip(0, e), "pair": 0})

    def inside(f, e, i):
        at = 2 * (4 * f + e) + i
        return copy(chip(f, e), half * i, half, in_send, in_recv, at, {"pair": other})

    def mates(e):
        return copy(chip(0, e), 0, slots, in_send, in_recv, 2 * e, {"pair": other})

    def index_to(m):
        return pltpu.make_async_remote_copy(
            src_ref=index_ref,
            dst_ref=slot_rows.at[me],
            send_sem=index_send.at[m],
            recv_sem=index_recv.at[m],
            device_id={"chan": around(m)},
        )

    def all_rows():
        return pltpu.make_async_remote_copy(
            src_ref=slot_rows,
            dst_ref=slot_rows,
            send_sem=index_send.at[0],
            recv_sem=index_recv.at[0],
            device_id={"pair": other},
        )

    def chosen_of(block, index):
        r_ids = lax.broadcasted_iota(jnp.int32, (slots, slots), 0)
        k_ids = lax.broadcasted_iota(jnp.int32, (slots, slots), 1)
        return jnp.where((index == r_ids) & (k_ids < count_ref[block]), 1.0, 0.0)

    def send_index():
        for small in small_loads:
            small.wait()
        for m in range(1, n):
            index_to(m).start()
        slot_rows[me] = index_ref[...]

    def choose_all():
        none = jnp.zeros((slots, slots), jnp.bfloat16)
        for b in range(n // 2):
            left = chosen_of(2 * b, slot_rows[2 * b]).astype(jnp.bfloat16)
            right = chosen_of(2 * b + 1, slot_rows[2 * b + 1]).astype(jnp.bfloat16)
            chosen_ref[b, 0:slots, :] = jnp.concatenate([left, none], axis=1)
            chosen_ref[b, slots:, :] = jnp.concatenate([none, right], axis=1)

    def lag_rows():
        pick = chosen_of(me, index_ref[...]).T.astype(jnp.bfloat16)
        block = spread_ref[pl.ds(pl.multiple_of(me * slots, slots), slots), :]
        own = jnp.dot(pick, block, preferred_element_type=jnp.float32)
        weights = lag_ref[pl.ds(pl.multiple_of(8 * core, 8), 8), :]
        for l in range(L // 2):
            weight = weights[l : l + 1, :]
            lagged_ref[slots * l : slots * (l + 1), :] = (own * weight).astype(jnp.bfloat16)

    def correlate(f, e):
        at = pl.multiple_of(chip(f, e) // 2 * 2 * slots, 2 * slots)
        product = lax.dot_general(
            lagged_ref[...],
            spread_ref[pl.ds(at, 2 * slots), :],
            (((1,), (1,)), ((), ())),
            preferred_element_type=jnp.float32,
        ).astype(jnp.bfloat16)
        product = jnp.dot(
            product, chosen_ref[chip(f, e) // 2], preferred_element_type=jnp.float32
        ).astype(jnp.bfloat16)
        for l in range(L // 2):
            out_ref[l, :, pl.ds(at, 2 * slots)] = product[slots * l : slots * (l + 1)]

    @pl.when(core == 0)
    def _():
        pl.semaphore_wait(barrier, quads + 3)
        for f in fars:
            far(f, 0, me).start()
        for e in (1, 3, 2):
            mine(e, 0).start()
        inside(0, 0, 0).start()
        for small in small_loads:
            small.wait()
        inside(0, 0, 1).wait_recv()
        lag_rows()
        for e in (1, 3, 2):
            for i in (0, 1):
                mine(e, i).wait_recv()
            mates(e).start()
        all_rows().wait_recv()
        choose_all()
        correlate(0, 0)
        correlate(0, 2)
        for f in fars:
            for pair in ((0, 1), (2, 3)):
                for e in pair:
                    for i in (1, 0):
                        inside(f, e, i).wait_recv()
                correlate(f, pair[0])
        inside(0, 0, 0).wait_send()
        for f in fars:
            far(f, 0, me).wait_send()
        for e in (1, 3, 2):
            mine(e, 0).wait_send()
            mates(e).wait_send()

    @pl.when(core == 1)
    def _():
        pl.semaphore_wait(barrier, n + 6)
        for f in fars:
            far(f, 1, me).start()
        for e in (1, 3, 2):
            mine(e, 1).start()
        inside(0, 0, 1).start()
        send_index()
        for f in fars:
            for i in (1, 0):
                far(f, i, me).wait_recv()
                for e in (3, 2, 1):
                    near(f, e, i, chip(f, 0)).start()
                inside(f, 0, i).start()
        inside(0, 0, 0).wait_recv()
        lag_rows()
        for m in range(1, n):
            index_to(m).wait_recv()
        all_rows().start()
        choose_all()
        for f in fars:
            for i in (1, 0):
                for e in (1, 2, 3):
                    near(f, e, i, me).wait_recv()
                    inside(f, e, i).start()
            correlate(f, 0)
            correlate(f, 2)
        for e in (1, 3, 2):
            mates(e).wait_recv()
        correlate(0, 0)
        correlate(0, 2)
        inside(0, 0, 1).wait_send()
        for e in (1, 3, 2):
            mine(e, 1).wait_send()
        for f in fars:
            far(f, 1, me).wait_send()
            for i in (1, 0):
                for e in (1, 2, 3):
                    near(f, e, i, me).wait_send()
                    inside(f, e, i).wait_send()
                inside(f, 0, i).wait_send()
        all_rows().wait_send()
        for m in range(1, n):
            index_to(m).wait_send()


def shards(n, raw, live_index, live_count):
    slots = raw.shape[0]
    vmem = pl.BlockSpec(memory_space=pltpu.VMEM)
    return pl.pallas_call(
        functools.partial(kernel, n),
        out_shape=pltpu.VMEM((L // 2, slots, n * slots), jnp.bfloat16),
        in_specs=[
            pl.BlockSpec(memory_space=pl.ANY),
            pl.BlockSpec(memory_space=pl.ANY),
            pl.BlockSpec(memory_space=pl.ANY),
            pl.BlockSpec(memory_space=pl.ANY),
            pl.BlockSpec(memory_space=pl.ANY),
        ],
        out_specs=vmem,
        scratch_shapes=[
            pltpu.VMEM((1, slots), jnp.int32),
            pltpu.SMEM((n,), jnp.int32),
            pltpu.VMEM((16, COLS), jnp.float32),
            pltpu.VMEM((BASE, COLS + 128), jnp.float32),
            pltpu.VMEM((slots // 2, S), jnp.bfloat16),
            pltpu.VMEM((2 * slots, KROWS), jnp.bfloat16),
            pltpu.VMEM((KROWS, COLS), jnp.bfloat16),
            pltpu.VMEM((2 * slots, COLS), jnp.float32),
            pltpu.VMEM((n * slots, COLS), jnp.bfloat16),
            pltpu.VMEM((L // 2 * slots, COLS), jnp.bfloat16),
            pltpu.VMEM((n, 1, slots), jnp.int32),
            pltpu.VMEM((n // 2, 2 * slots, 2 * slots), jnp.bfloat16),
            pltpu.SemaphoreType.DMA,
            pltpu.SemaphoreType.DMA((3,)),
            pltpu.SemaphoreType.DMA,
            pltpu.SemaphoreType.DMA((n // 2,)),
            pltpu.SemaphoreType.DMA((n // 2,)),
            pltpu.SemaphoreType.DMA((2 * n,)),
            pltpu.SemaphoreType.DMA((2 * n,)),
            pltpu.SemaphoreType.DMA((2 * n,)),
            pltpu.SemaphoreType.DMA((2 * n,)),
            pltpu.SemaphoreType.DMA((n,)),
            pltpu.SemaphoreType.DMA((n,)),
        ],
        compiler_params=pltpu.CompilerParams(
            collective_id=0, has_side_effects=True, vmem_limit_bytes=VMEM_LIMIT - 6 * slots * n * slots
        ),
    )(
        raw.reshape(slots, S),
        live_index,
        live_count,
        jnp.asarray(dft_table(), jnp.bfloat16),
        jnp.asarray(lag_table()),
    )


def solution(mesh):
    return jax.shard_map(
        functools.partial(shards, mesh.shape["chan"]),
        mesh=mesh,
        in_specs=(P(("groups", "chan"), None, None), P(("groups", "chan"), None), P("groups")),
        out_specs=P("pair", ("groups", "chan"), None),
        check_vma=False,
    )
```

```python
import functools

import jax
import jax.numpy as jnp
import numpy as np
from jax import lax
from jax.experimental import pallas as pl
from jax.experimental.pallas import tpu as pltpu
from jax.sharding import PartitionSpec as P

S = 12000
NB = 448
L = 6
LSTEP = 125
F0 = 60
WATER = 0.1
QUARTER = S // 4
BASE = 128
BASE_STEP = 32
PAIRS = 7
MADE = 2 * BASE * PAIRS
KROWS = 3072
TROWS = 3008
FULL = NB // 128
TAIL = NB - 128 * FULL
COLS = 2 * NB
VMEM_LIMIT = 63_300_000


def column_bins():
    full = np.arange(128 * FULL).reshape(FULL, 1, 128)
    tail = np.arange(128 * FULL, NB)
    return np.concatenate([np.repeat(full, 2, axis=1).reshape(-1), tail, tail])


def column_is_sine():
    full = np.repeat(np.arange(2) == 1, 128)
    return np.concatenate([np.tile(full, FULL), np.repeat(np.arange(2) == 1, TAIL)])


def dft_table():
    phase = np.arange(MADE, QUARTER)[:, None] * (F0 + column_bins())[None, :] % S
    angle = (phase.astype(np.float32) * np.float32(2.0 * np.pi / S)).astype(np.float64)
    out = np.zeros((TROWS - MADE, COLS), np.float32)
    out[: QUARTER - MADE] = np.where(column_is_sine()[None, :], -np.sin(angle), np.cos(angle))
    return out


def lag_table():
    j = column_bins()
    taper = 0.5 - 0.5 * np.cos(2.0 * np.pi * (j + 0.5) / NB)
    lags = np.arange(L)[:, None] * LSTEP
    waves = np.cos(2.0 * np.pi * (((F0 + j)[None, :] * lags) % S) / S)
    table = np.zeros((2, 8, COLS), np.float32)
    table[:, : L // 2] = (taper[None, :] * waves / np.sqrt(NB)).reshape(2, L // 2, COLS)
    return table.reshape(16, COLS)


def cosine_and_minus_sine(step, bins, shift=0.0):
    phase = step * (bins + F0)
    turns = jnp.floor(phase * (4.0 / S) + 0.5)
    x = (phase - turns * (S / 4)) * (2.0 * np.pi / S) + shift
    y = x * x
    c = 1.0 + y * (-0.5 + y * (1 / 24 + y * (-1 / 720 + y * (1 / 40320))))
    s = -x * (1.0 + y * (-1 / 6 + y * (1 / 120 + y * (-1 / 5040 + y * (1 / 362880)))))
    turns = turns - 4.0 * jnp.floor(turns * 0.25)
    odd = (turns == 1.0) | (turns == 3.0)
    cosine, minus_sine = jnp.where(odd, s, c), jnp.where(odd, -c, s)
    back = turns >= 2.0
    return jnp.where(back, -cosine, cosine), jnp.where(back, -minus_sine, minus_sine)


def lane_bins(rows, v):
    lane = lax.broadcasted_iota(jnp.int32, (rows, 128), 1)
    if v == FULL:
        lane = jnp.where(lane < TAIL, lane, lane - TAIL)
    return (lane + 128 * v).astype(jnp.float32)


def make_base(rot_ref):
    unit = 2.0 * np.pi / S
    shift = np.pi * (float(np.float32(unit)) / unit - 1.0)
    cosine = lax.broadcasted_iota(jnp.int32, (BASE_STEP, 128), 1) < TAIL

    def rows_of(i, carry):
        at = pl.ds(pl.multiple_of(i * BASE_STEP, BASE_STEP), BASE_STEP)
        row = lax.broadcasted_iota(jnp.int32, (BASE_STEP, 128), 0) + i * BASE_STEP
        step = (row + (BASE * PAIRS - BASE // 2)).astype(jnp.float32)
        for v in range(FULL + 1):
            c, s = cosine_and_minus_sine(step, lane_bins(BASE_STEP, v), shift)
            if v == FULL:
                c, s = jnp.where(cosine, c, s), jnp.where(cosine, s, c)
            rot_ref[at, 256 * v : 256 * v + 128] = c
            rot_ref[at, 256 * v + 128 : 256 * v + 256] = s
        return carry

    lax.fori_loop(0, BASE // BASE_STEP, rows_of, 0)


def make_rows(rot_ref, table_ref):
    cosine = lax.broadcasted_iota(jnp.int32, (8, 128), 1) < TAIL

    def pair(m, carry):
        step = (jnp.full((8, 128), BASE // 2, jnp.int32) * (2 * m + 1)).astype(jnp.float32)
        above = pl.multiple_of(BASE * (PAIRS + m), BASE)
        below = pl.multiple_of(BASE * (PAIRS - 1 - m), BASE)
        for v in range(FULL + 1):
            one, two = slice(256 * v, 256 * v + 128), slice(256 * v + 128, 256 * v + 256)
            turn_c, turn_s = cosine_and_minus_sine(step, lane_bins(8, v))
            if v == FULL:
                turn_s = jnp.where(cosine, -turn_s, turn_s)
            turn_c = jnp.concatenate([turn_c] * 2, axis=0)
            turn_s = jnp.concatenate([turn_s] * 2, axis=0)
            for r in range(0, BASE, 16):
                c, s = rot_ref[r : r + 16, one], rot_ref[r : r + 16, two]
                cc, ss = c * turn_c, s * turn_s
                up, down = pl.ds(above + r, 16), pl.ds(below + r, 16)
                if v < FULL:
                    sc, cs = s * turn_c, c * turn_s
                    table_ref[up, one] = (cc - ss).astype(jnp.bfloat16)
                    table_ref[down, one] = (cc + ss).astype(jnp.bfloat16)
                    table_ref[up, two] = (sc + cs).astype(jnp.bfloat16)
                    table_ref[down, two] = (sc - cs).astype(jnp.bfloat16)
                else:
                    table_ref[up, one] = (cc + ss).astype(jnp.bfloat16)
                    table_ref[down, one] = (cc - ss).astype(jnp.bfloat16)
        return carry

    lax.fori_loop(0, PAIRS, pair, 0)


def lane_signs(slots, first):
    m = (lax.broadcasted_iota(jnp.int32, (slots, 128), 1) + first) % 4
    return m % 2 == 0, jnp.where(m < 2, 1.0, -1.0)


def combine(spec, slots):
    a = [spec[slots * q : slots * (q + 1), 0:128] for q in range(4)]
    b = [spec[slots * q : slots * (q + 1), 128:256] for q in range(4)]
    even, sign = lane_signs(slots, F0)
    re = jnp.where(even, a[0] + a[2] + sign * (a[1] + a[3]), a[0] - a[2] + sign * (b[1] - b[3]))
    im = jnp.where(even, b[0] + b[2] + sign * (b[1] + b[3]), b[0] - b[2] - sign * (a[1] - a[3]))
    return re, im


def combine_tail(spec, slots):
    v = [spec[slots * q : slots * (q + 1), :] for q in range(4)]
    even, sign = lane_signs(slots, F0)
    real = lax.broadcasted_iota(jnp.int32, (slots, 128), 1) < TAIL
    turned = jnp.where(real, sign, -sign) * pltpu.roll(v[1] - v[3], TAIL, 1)
    return jnp.where(even, v[0] + v[2] + sign * (v[1] + v[3]), v[0] - v[2] + turned)


def kernel(
    n,
    raw_hbm,
    index_hbm,
    count_hbm,
    table_hbm,
    lag_hbm,
    out_ref,
    index_ref,
    count_ref,
    lag_ref,
    rot_ref,
    x_ref,
    xq_ref,
    table_ref,
    spec_ref,
    spread_ref,
    lagged_ref,
    slot_rows,
    chosen_ref,
    load_sem,
    small_sem,
    table_sem,
    far_send,
    far_recv,
    near_send,
    near_recv,
    in_send,
    in_recv,
    index_send,
    index_recv,
):
    slots = raw_hbm.shape[0]
    half = slots // 2
    me = lax.axis_index("chan")
    core = lax.axis_index("pair")
    other = 1 - core

    first = pl.multiple_of(core * half, half)
    load = pltpu.make_async_copy(raw_hbm.at[pl.ds(first, half)], x_ref, load_sem)
    load.start()
    small_loads = [
        pltpu.make_async_copy(index_hbm, index_ref, small_sem.at[0]),
        pltpu.make_async_copy(count_hbm, count_ref, small_sem.at[1]),
        pltpu.make_async_copy(lag_hbm, lag_ref, small_sem.at[2]),
    ]
    table_load = pltpu.make_async_copy(table_hbm, table_ref.at[MADE:TROWS], table_sem)
    for small in small_loads:
        small.start()
    table_load.start()

    quads = n // 4
    quad, corner = me // 4, lax.rem(me, 4)
    fars = list(range(1, quads))

    def flip(value, mask):
        for bit in range(mask.bit_length()):
            if mask >> bit & 1:
                value = value + (1 << bit) - (2 << bit) * lax.rem(value // (1 << bit), 2)
        return value

    def chip(f, e):
        return 4 * flip(quad, f) + flip(corner, e)

    def around(m):
        return lax.rem(me + m, n)

    barrier = pltpu.get_barrier_semaphore()
    pl.semaphore_signal(barrier, inc=1, device_id={"pair": other})
    for e in (1, 2, 3):
        pl.semaphore_signal(barrier, inc=1, device_id={"chan": chip(0, e)})

    @pl.when(core == 0)
    def _():
        for e in (1, 2, 3):
            pl.semaphore_signal(barrier, inc=1, device_id={"chan": chip(0, e), "pair": 1})

    @pl.when(core == 1)
    def _():
        for m in range(1, n):
            pl.semaphore_signal(barrier, inc=1, device_id={"chan": around(m)})
        for f in fars:
            pl.semaphore_signal(barrier, inc=1, device_id={"chan": chip(f, 0), "pair": 0})

    make_base(rot_ref)
    make_rows(rot_ref, table_ref)
    table_ref[TROWS:, :] = jnp.zeros((KROWS - TROWS, COLS), jnp.bfloat16)
    load.wait()
    for q in range(4):
        rows = slice(half * q, half * (q + 1))
        xq_ref[rows, 0:QUARTER] = x_ref[:, QUARTER * q : QUARTER * (q + 1)]
        xq_ref[rows, QUARTER:] = jnp.zeros((half, KROWS - QUARTER), jnp.bfloat16)

    spectrum = jnp.dot(xq_ref[:, :MADE], table_ref[:MADE, :], preferred_element_type=jnp.float32)
    spec_ref[...] = spectrum
    table_load.wait()
    spectrum = spec_ref[...] + jnp.dot(
        xq_ref[:, MADE:], table_ref[MADE:, :], preferred_element_type=jnp.float32
    )

    parts, power = [], jnp.zeros((half, 1), jnp.float32)
    for j in range(FULL + 1):
        spec = spectrum[:, 256 * j : 256 * j + 256]
        if j < FULL:
            re, im = combine(spec, half)
            mag = re * re + im * im
            power = power + jnp.sum(mag, axis=1, keepdims=True)
        else:
            both = combine_tail(spec, half)
            square = both * both
            mag = square + pltpu.roll(square, TAIL, 1)
            power = power + jnp.sum(square, axis=1, keepdims=True)
        parts.append((re, im, mag) if j < FULL else (both, None, mag))
    floor = power * (WATER / NB) + 1e-06
    whitened = []
    for re, im, mag in parts:
        scale = lax.rsqrt(mag + floor)
        whitened.append(re * scale)
        if im is not None:
            whitened.append(im * scale)
    whitened = jnp.concatenate(whitened, axis=1).astype(jnp.bfloat16)

    spread_ref[pl.ds(pl.multiple_of(me * slots + first, half), half), :] = whitened

    def copy(block, first, rows, sends, recvs, at, device_id):
        ref = spread_ref.at[pl.ds(pl.multiple_of(block * slots + first, rows), rows), :]
        return pltpu.make_async_remote_copy(
            src_ref=ref,
            dst_ref=ref,
            send_sem=sends.at[at],
            recv_sem=recvs.at[at],
            device_id=device_id,
        )

    def far(f, i, block):
        at = 2 * f + i
        return copy(block, half * i, half, far_send, far_recv, at, {"chan": chip(f, 0), "pair": 1})

    def near(f, e, i, block):
        at = 2 * (4 * f + e) + i
        return copy(block, half * i, half, near_send, near_recv, at, {"chan": chip(0, e)})

    def mine(e, i):
        at = 2 * e + i
        return copy(me, half * i, half, near_send, near_recv, at, {"chan": chip(0, e), "pair": 0})

    def inside(f, e, i):
        at = 2 * (4 * f + e) + i
        return copy(chip(f, e), half * i, half, in_send, in_recv, at, {"pair": other})

    def mates(e):
        return copy(chip(0, e), 0, slots, in_send, in_recv, 2 * e, {"pair": other})

    def index_to(m):
        return pltpu.make_async_remote_copy(
            src_ref=index_ref,
            dst_ref=slot_rows.at[me],
            send_sem=index_send.at[m],
            recv_sem=index_recv.at[m],
            device_id={"chan": around(m)},
        )

    def all_rows():
        return pltpu.make_async_remote_copy(
            src_ref=slot_rows,
            dst_ref=slot_rows,
            send_sem=index_send.at[0],
            recv_sem=index_recv.at[0],
            device_id={"pair": other},
        )

    def chosen_of(block, index):
        r_ids = lax.broadcasted_iota(jnp.int32, (slots, slots), 0)
        k_ids = lax.broadcasted_iota(jnp.int32, (slots, slots), 1)
        return jnp.where((index == r_ids) & (k_ids < count_ref[block]), 1.0, 0.0)

    def send_index():
        for small in small_loads:
            small.wait()
        for m in range(1, n):
            index_to(m).start()
        slot_rows[me] = index_ref[...]

    def choose_all():
        none = jnp.zeros((slots, slots), jnp.bfloat16)
        for b in range(n // 2):
            left = chosen_of(2 * b, slot_rows[2 * b]).astype(jnp.bfloat16)
            right = chosen_of(2 * b + 1, slot_rows[2 * b + 1]).astype(jnp.bfloat16)
            chosen_ref[b, 0:slots, :] = jnp.concatenate([left, none], axis=1)
            chosen_ref[b, slots:, :] = jnp.concatenate([none, right], axis=1)

    def lag_rows():
        pick = chosen_of(me, index_ref[...]).T.astype(jnp.bfloat16)
        block = spread_ref[pl.ds(pl.multiple_of(me * slots, slots), slots), :]
        own = jnp.dot(pick, block, preferred_element_type=jnp.float32)
        weights = lag_ref[pl.ds(pl.multiple_of(8 * core, 8), 8), :]
        for l in range(L // 2):
            weight = weights[l : l + 1, :]
            lagged_ref[slots * l : slots * (l + 1), :] = (own * weight).astype(jnp.bfloat16)

    def correlate(f, e):
        at = pl.multiple_of(chip(f, e) // 2 * 2 * slots, 2 * slots)
        product = lax.dot_general(
            lagged_ref[...],
            spread_ref[pl.ds(at, 2 * slots), :],
            (((1,), (1,)), ((), ())),
            preferred_element_type=jnp.float32,
        ).astype(jnp.bfloat16)
        product = jnp.dot(
            product, chosen_ref[chip(f, e) // 2], preferred_element_type=jnp.float32
        ).astype(jnp.bfloat16)
        for l in range(L // 2):
            out_ref[l, :, pl.ds(at, 2 * slots)] = product[slots * l : slots * (l + 1)]

    @pl.when(core == 0)
    def _():
        pl.semaphore_wait(barrier, quads + 3)
        for f in fars:
            far(f, 0, me).start()
        for e in (1, 3, 2):
            mine(e, 0).start()
        inside(0, 0, 0).start()
        for small in small_loads:
            small.wait()
        inside(0, 0, 1).wait_recv()
        lag_rows()
        for e in (1, 3, 2):
            for i in (0, 1):
                mine(e, i).wait_recv()
            mates(e).start()
        all_rows().wait_recv()
        choose_all()
        correlate(0, 0)
        correlate(0, 2)
        for f in fars:
            for pair in ((0, 1), (2, 3)):
                for e in pair:
                    for i in (1, 0):
                        inside(f, e, i).wait_recv()
                correlate(f, pair[0])
        inside(0, 0, 0).wait_send()
        for f in fars:
            far(f, 0, me).wait_send()
        for e in (1, 3, 2):
            mine(e, 0).wait_send()
            mates(e).wait_send()

    @pl.when(core == 1)
    def _():
        pl.semaphore_wait(barrier, n + 6)
        for f in fars:
            far(f, 1, me).start()
        for e in (1, 3, 2):
            mine(e, 1).start()
        inside(0, 0, 1).start()
        send_index()
        for f in fars:
            for i in (1, 0):
                far(f, i, me).wait_recv()
                for e in (3, 1, 2):
                    near(f, e, i, chip(f, 0)).start()
                inside(f, 0, i).start()
        inside(0, 0, 0).wait_recv()
        lag_rows()
        for f in fars:
            for e in (1, 2, 3):
                near(f, e, 1, me).wait_recv()
                inside(f, e, 1).start()
        for m in range(1, n):
            index_to(m).wait_recv()
        all_rows().start()
        choose_all()
        for f in fars:
            for e in (1, 2, 3):
                near(f, e, 0, me).wait_recv()
                inside(f, e, 0).start()
            correlate(f, 0)
            correlate(f, 2)
        for e in (1, 3, 2):
            mates(e).wait_recv()
        correlate(0, 0)
        correlate(0, 2)
        inside(0, 0, 1).wait_send()
        for e in (1, 3, 2):
            mine(e, 1).wait_send()
        for f in fars:
            far(f, 1, me).wait_send()
            for i in (1, 0):
                for e in (1, 2, 3):
                    near(f, e, i, me).wait_send()
                    inside(f, e, i).wait_send()
                inside(f, 0, i).wait_send()
        all_rows().wait_send()
        for m in range(1, n):
            index_to(m).wait_send()


def shards(n, raw, live_index, live_count):
    slots = raw.shape[0]
    vmem = pl.BlockSpec(memory_space=pltpu.VMEM)
    return pl.pallas_call(
        functools.partial(kernel, n),
        out_shape=pltpu.VMEM((L // 2, slots, n * slots), jnp.bfloat16),
        in_specs=[
            pl.BlockSpec(memory_space=pl.ANY),
            pl.BlockSpec(memory_space=pl.ANY),
            pl.BlockSpec(memory_space=pl.ANY),
            pl.BlockSpec(memory_space=pl.ANY),
            pl.BlockSpec(memory_space=pl.ANY),
        ],
        out_specs=vmem,
        scratch_shapes=[
            pltpu.VMEM((1, slots), jnp.int32),
            pltpu.SMEM((n,), jnp.int32),
            pltpu.VMEM((16, COLS), jnp.float32),
            pltpu.VMEM((BASE, COLS + 128), jnp.float32),
            pltpu.VMEM((slots // 2, S), jnp.bfloat16),
            pltpu.VMEM((2 * slots, KROWS), jnp.bfloat16),
            pltpu.VMEM((KROWS, COLS), jnp.bfloat16),
            pltpu.VMEM((2 * slots, COLS), jnp.float32),
            pltpu.VMEM((n * slots, COLS), jnp.bfloat16),
            pltpu.VMEM((L // 2 * slots, COLS), jnp.bfloat16),
            pltpu.VMEM((n, 1, slots), jnp.int32),
            pltpu.VMEM((n // 2, 2 * slots, 2 * slots), jnp.bfloat16),
            pltpu.SemaphoreType.DMA,
            pltpu.SemaphoreType.DMA((3,)),
            pltpu.SemaphoreType.DMA,
            pltpu.SemaphoreType.DMA((n // 2,)),
            pltpu.SemaphoreType.DMA((n // 2,)),
            pltpu.SemaphoreType.DMA((2 * n,)),
            pltpu.SemaphoreType.DMA((2 * n,)),
            pltpu.SemaphoreType.DMA((2 * n,)),
            pltpu.SemaphoreType.DMA((2 * n,)),
            pltpu.SemaphoreType.DMA((n,)),
            pltpu.SemaphoreType.DMA((n,)),
        ],
        compiler_params=pltpu.CompilerParams(
            collective_id=0, has_side_effects=True, vmem_limit_bytes=VMEM_LIMIT - 6 * slots * n * slots
        ),
    )(
        raw.reshape(slots, S),
        live_index,
        live_count,
        jnp.asarray(dft_table(), jnp.bfloat16),
        jnp.asarray(lag_table()),
    )


def solution(mesh):
    return jax.shard_map(
        functools.partial(shards, mesh.shape["chan"]),
        mesh=mesh,
        in_specs=(P(("groups", "chan"), None, None), P(("groups", "chan"), None), P("groups")),
        out_specs=P("pair", ("groups", "chan"), None),
        check_vma=False,
    )
```

```python
import functools

import jax
import jax.numpy as jnp
import numpy as np
from jax import lax
from jax.experimental import pallas as pl
from jax.experimental.pallas import tpu as pltpu
from jax.sharding import PartitionSpec as P

S = 12000
NB = 448
L = 6
LSTEP = 125
F0 = 60
WATER = 0.1
QUARTER = S // 4
BASE = 128
BASE_STEP = 32
PAIRS = 7
MADE = 2 * BASE * PAIRS
KROWS = 3072
TROWS = 3008
FULL = NB // 128
TAIL = NB - 128 * FULL
COLS = 2 * NB
VMEM_LIMIT = 63_300_000


def column_bins():
    full = np.arange(128 * FULL).reshape(FULL, 1, 128)
    tail = np.arange(128 * FULL, NB)
    return np.concatenate([np.repeat(full, 2, axis=1).reshape(-1), tail, tail])


def column_is_sine():
    full = np.repeat(np.arange(2) == 1, 128)
    return np.concatenate([np.tile(full, FULL), np.repeat(np.arange(2) == 1, TAIL)])


def dft_table():
    phase = np.arange(MADE, QUARTER)[:, None] * (F0 + column_bins())[None, :] % S
    angle = (phase.astype(np.float32) * np.float32(2.0 * np.pi / S)).astype(np.float64)
    out = np.zeros((TROWS - MADE, COLS), np.float32)
    out[: QUARTER - MADE] = np.where(column_is_sine()[None, :], -np.sin(angle), np.cos(angle))
    return out


def lag_table():
    j = column_bins()
    taper = 0.5 - 0.5 * np.cos(2.0 * np.pi * (j + 0.5) / NB)
    lags = np.arange(L)[:, None] * LSTEP
    waves = np.cos(2.0 * np.pi * (((F0 + j)[None, :] * lags) % S) / S)
    table = np.zeros((2, 8, COLS), np.float32)
    table[:, : L // 2] = (taper[None, :] * waves / np.sqrt(NB)).reshape(2, L // 2, COLS)
    return table.reshape(16, COLS)


def cosine_and_minus_sine(step, bins, shift=0.0):
    phase = step * (bins + F0)
    turns = jnp.floor(phase * (4.0 / S) + 0.5)
    x = (phase - turns * (S / 4)) * (2.0 * np.pi / S) + shift
    y = x * x
    c = 1.0 + y * (-0.5 + y * (1 / 24 + y * (-1 / 720 + y * (1 / 40320))))
    s = -x * (1.0 + y * (-1 / 6 + y * (1 / 120 + y * (-1 / 5040 + y * (1 / 362880)))))
    turns = turns - 4.0 * jnp.floor(turns * 0.25)
    odd = (turns == 1.0) | (turns == 3.0)
    cosine, minus_sine = jnp.where(odd, s, c), jnp.where(odd, -c, s)
    back = turns >= 2.0
    return jnp.where(back, -cosine, cosine), jnp.where(back, -minus_sine, minus_sine)


def lane_bins(rows, v):
    lane = lax.broadcasted_iota(jnp.int32, (rows, 128), 1)
    if v == FULL:
        lane = jnp.where(lane < TAIL, lane, lane - TAIL)
    return (lane + 128 * v).astype(jnp.float32)


def make_base(rot_ref):
    unit = 2.0 * np.pi / S
    shift = np.pi * (float(np.float32(unit)) / unit - 1.0)
    cosine = lax.broadcasted_iota(jnp.int32, (BASE_STEP, 128), 1) < TAIL

    def rows_of(i, carry):
        at = pl.ds(pl.multiple_of(i * BASE_STEP, BASE_STEP), BASE_STEP)
        row = lax.broadcasted_iota(jnp.int32, (BASE_STEP, 128), 0) + i * BASE_STEP
        step = (row + (BASE * PAIRS - BASE // 2)).astype(jnp.float32)
        for v in range(FULL + 1):
            c, s = cosine_and_minus_sine(step, lane_bins(BASE_STEP, v), shift)
            if v == FULL:
                c, s = jnp.where(cosine, c, s), jnp.where(cosine, s, c)
            rot_ref[at, 256 * v : 256 * v + 128] = c
            rot_ref[at, 256 * v + 128 : 256 * v + 256] = s
        return carry

    lax.fori_loop(0, BASE // BASE_STEP, rows_of, 0)


def make_rows(rot_ref, table_ref):
    cosine = lax.broadcasted_iota(jnp.int32, (8, 128), 1) < TAIL

    def pair(m, carry):
        step = (jnp.full((8, 128), BASE // 2, jnp.int32) * (2 * m + 1)).astype(jnp.float32)
        above = pl.multiple_of(BASE * (PAIRS + m), BASE)
        below = pl.multiple_of(BASE * (PAIRS - 1 - m), BASE)
        for v in range(FULL + 1):
            one, two = slice(256 * v, 256 * v + 128), slice(256 * v + 128, 256 * v + 256)
            turn_c, turn_s = cosine_and_minus_sine(step, lane_bins(8, v))
            if v == FULL:
                turn_s = jnp.where(cosine, -turn_s, turn_s)
            turn_c = jnp.concatenate([turn_c] * 2, axis=0)
            turn_s = jnp.concatenate([turn_s] * 2, axis=0)
            for r in range(0, BASE, 16):
                c, s = rot_ref[r : r + 16, one], rot_ref[r : r + 16, two]
                cc, ss = c * turn_c, s * turn_s
                up, down = pl.ds(above + r, 16), pl.ds(below + r, 16)
                if v < FULL:
                    sc, cs = s * turn_c, c * turn_s
                    table_ref[up, one] = (cc - ss).astype(jnp.bfloat16)
                    table_ref[down, one] = (cc + ss).astype(jnp.bfloat16)
                    table_ref[up, two] = (sc + cs).astype(jnp.bfloat16)
                    table_ref[down, two] = (sc - cs).astype(jnp.bfloat16)
                else:
                    table_ref[up, one] = (cc + ss).astype(jnp.bfloat16)
                    table_ref[down, one] = (cc - ss).astype(jnp.bfloat16)
        return carry

    lax.fori_loop(0, PAIRS, pair, 0)


def lane_signs(slots, first):
    m = (lax.broadcasted_iota(jnp.int32, (slots, 128), 1) + first) % 4
    return m % 2 == 0, jnp.where(m < 2, 1.0, -1.0)


def combine(spec, slots):
    a = [spec[slots * q : slots * (q + 1), 0:128] for q in range(4)]
    b = [spec[slots * q : slots * (q + 1), 128:256] for q in range(4)]
    even, sign = lane_signs(slots, F0)
    re = jnp.where(even, a[0] + a[2] + sign * (a[1] + a[3]), a[0] - a[2] + sign * (b[1] - b[3]))
    im = jnp.where(even, b[0] + b[2] + sign * (b[1] + b[3]), b[0] - b[2] - sign * (a[1] - a[3]))
    return re, im


def combine_tail(spec, slots):
    v = [spec[slots * q : slots * (q + 1), :] for q in range(4)]
    even, sign = lane_signs(slots, F0)
    real = lax.broadcasted_iota(jnp.int32, (slots, 128), 1) < TAIL
    turned = jnp.where(real, sign, -sign) * pltpu.roll(v[1] - v[3], TAIL, 1)
    return jnp.where(even, v[0] + v[2] + sign * (v[1] + v[3]), v[0] - v[2] + turned)


def kernel(
    n,
    raw_hbm,
    index_hbm,
    count_hbm,
    table_hbm,
    lag_hbm,
    out_ref,
    index_ref,
    count_ref,
    lag_ref,
    rot_ref,
    x_ref,
    xq_ref,
    table_ref,
    spec_ref,
    spread_ref,
    lagged_ref,
    slot_rows,
    chosen_ref,
    load_sem,
    small_sem,
    table_sem,
    far_send,
    far_recv,
    near_send,
    near_recv,
    in_send,
    in_recv,
    index_send,
    index_recv,
):
    slots = raw_hbm.shape[0]
    half = slots // 2
    me = lax.axis_index("chan")
    core = lax.axis_index("pair")
    other = 1 - core

    first = pl.multiple_of(core * half, half)
    load = pltpu.make_async_copy(raw_hbm.at[pl.ds(first, half)], x_ref, load_sem)
    load.start()
    small_loads = [
        pltpu.make_async_copy(index_hbm, index_ref, small_sem.at[0]),
        pltpu.make_async_copy(count_hbm, count_ref, small_sem.at[1]),
        pltpu.make_async_copy(lag_hbm, lag_ref, small_sem.at[2]),
    ]
    table_load = pltpu.make_async_copy(table_hbm, table_ref.at[MADE:TROWS], table_sem)
    for small in small_loads:
        small.start()
    table_load.start()

    quads = n // 4
    quad, corner = me // 4, lax.rem(me, 4)
    fars = list(range(1, quads))

    def flip(value, mask):
        for bit in range(mask.bit_length()):
            if mask >> bit & 1:
                value = value + (1 << bit) - (2 << bit) * lax.rem(value // (1 << bit), 2)
        return value

    def chip(f, e):
        return 4 * flip(quad, f) + flip(corner, e)

    def around(m):
        return lax.rem(me + m, n)

    barrier = pltpu.get_barrier_semaphore()
    pl.semaphore_signal(barrier, inc=1, device_id={"pair": other})
    for e in (1, 2, 3):
        pl.semaphore_signal(barrier, inc=1, device_id={"chan": chip(0, e)})

    @pl.when(core == 0)
    def _():
        for e in (1, 2, 3):
            pl.semaphore_signal(barrier, inc=1, device_id={"chan": chip(0, e), "pair": 1})

    @pl.when(core == 1)
    def _():
        for m in range(1, n):
            pl.semaphore_signal(barrier, inc=1, device_id={"chan": around(m)})
        for f in fars:
            pl.semaphore_signal(barrier, inc=1, device_id={"chan": chip(f, 0), "pair": 0})

    make_base(rot_ref)
    make_rows(rot_ref, table_ref)
    table_ref[TROWS:, :] = jnp.zeros((KROWS - TROWS, COLS), jnp.bfloat16)
    load.wait()
    for q in range(4):
        rows = slice(half * q, half * (q + 1))
        xq_ref[rows, 0:QUARTER] = x_ref[:, QUARTER * q : QUARTER * (q + 1)]
        xq_ref[rows, QUARTER:] = jnp.zeros((half, KROWS - QUARTER), jnp.bfloat16)

    spectrum = jnp.dot(xq_ref[:, :MADE], table_ref[:MADE, :], preferred_element_type=jnp.float32)
    spec_ref[...] = spectrum
    table_load.wait()
    spectrum = spec_ref[...] + jnp.dot(
        xq_ref[:, MADE:], table_ref[MADE:, :], preferred_element_type=jnp.float32
    )

    parts, power = [], jnp.zeros((half, 1), jnp.float32)
    for j in range(FULL + 1):
        spec = spectrum[:, 256 * j : 256 * j + 256]
        if j < FULL:
            re, im = combine(spec, half)
            mag = re * re + im * im
            power = power + jnp.sum(mag, axis=1, keepdims=True)
        else:
            both = combine_tail(spec, half)
            square = both * both
            mag = square + pltpu.roll(square, TAIL, 1)
            power = power + jnp.sum(square, axis=1, keepdims=True)
        parts.append((re, im, mag) if j < FULL else (both, None, mag))
    floor = power * (WATER / NB) + 1e-06
    whitened = []
    for re, im, mag in parts:
        scale = lax.rsqrt(mag + floor)
        whitened.append(re * scale)
        if im is not None:
            whitened.append(im * scale)
    whitened = jnp.concatenate(whitened, axis=1).astype(jnp.bfloat16)

    spread_ref[pl.ds(pl.multiple_of(me * slots + first, half), half), :] = whitened

    def copy(block, first, rows, sends, recvs, at, device_id):
        ref = spread_ref.at[pl.ds(pl.multiple_of(block * slots + first, rows), rows), :]
        return pltpu.make_async_remote_copy(
            src_ref=ref,
            dst_ref=ref,
            send_sem=sends.at[at],
            recv_sem=recvs.at[at],
            device_id=device_id,
        )

    def far(f, i, block):
        at = 2 * f + i
        return copy(block, half * i, half, far_send, far_recv, at, {"chan": chip(f, 0), "pair": 1})

    def near(f, e, i, block):
        at = 2 * (4 * f + e) + i
        return copy(block, half * i, half, near_send, near_recv, at, {"chan": chip(0, e)})

    def mine(e, i):
        at = 2 * e + i
        return copy(me, half * i, half, near_send, near_recv, at, {"chan": chip(0, e), "pair": 0})

    def inside(f, e, i):
        at = 2 * (4 * f + e) + i
        return copy(chip(f, e), half * i, half, in_send, in_recv, at, {"pair": other})

    def mates(e):
        return copy(chip(0, e), 0, slots, in_send, in_recv, 2 * e, {"pair": other})

    def index_to(m):
        return pltpu.make_async_remote_copy(
            src_ref=index_ref,
            dst_ref=slot_rows.at[me],
            send_sem=index_send.at[m],
            recv_sem=index_recv.at[m],
            device_id={"chan": around(m)},
        )

    def all_rows():
        return pltpu.make_async_remote_copy(
            src_ref=slot_rows,
            dst_ref=slot_rows,
            send_sem=index_send.at[0],
            recv_sem=index_recv.at[0],
            device_id={"pair": other},
        )

    def chosen_of(block, index):
        r_ids = lax.broadcasted_iota(jnp.int32, (slots, slots), 0)
        k_ids = lax.broadcasted_iota(jnp.int32, (slots, slots), 1)
        return jnp.where((index == r_ids) & (k_ids < count_ref[block]), 1.0, 0.0)

    def send_index():
        for small in small_loads:
            small.wait()
        for m in range(1, n):
            index_to(m).start()
        slot_rows[me] = index_ref[...]

    def choose_all():
        none = jnp.zeros((slots, slots), jnp.bfloat16)
        for b in range(n // 2):
            left = chosen_of(2 * b, slot_rows[2 * b]).astype(jnp.bfloat16)
            right = chosen_of(2 * b + 1, slot_rows[2 * b + 1]).astype(jnp.bfloat16)
            chosen_ref[b, 0:slots, :] = jnp.concatenate([left, none], axis=1)
            chosen_ref[b, slots:, :] = jnp.concatenate([none, right], axis=1)

    def lag_rows():
        pick = chosen_of(me, index_ref[...]).T.astype(jnp.bfloat16)
        block = spread_ref[pl.ds(pl.multiple_of(me * slots, slots), slots), :]
        own = jnp.dot(pick, block, preferred_element_type=jnp.float32)
        weights = lag_ref[pl.ds(pl.multiple_of(8 * core, 8), 8), :]
        for l in range(L // 2):
            weight = weights[l : l + 1, :]
            lagged_ref[slots * l : slots * (l + 1), :] = (own * weight).astype(jnp.bfloat16)

    def correlate(f, e):
        at = pl.multiple_of(chip(f, e) // 2 * 2 * slots, 2 * slots)
        product = lax.dot_general(
            lagged_ref[...],
            spread_ref[pl.ds(at, 2 * slots), :],
            (((1,), (1,)), ((), ())),
            preferred_element_type=jnp.float32,
        ).astype(jnp.bfloat16)
        product = jnp.dot(
            product, chosen_ref[chip(f, e) // 2], preferred_element_type=jnp.float32
        ).astype(jnp.bfloat16)
        for l in range(L // 2):
            out_ref[l, :, pl.ds(at, 2 * slots)] = product[slots * l : slots * (l + 1)]

    @pl.when(core == 0)
    def _():
        pl.semaphore_wait(barrier, quads + 3)
        for f in fars:
            far(f, 0, me).start()
        for e in (1, 3, 2):
            mine(e, 0).start()
        inside(0, 0, 0).start()
        for small in small_loads:
            small.wait()
        inside(0, 0, 1).wait_recv()
        lag_rows()
        for e in (1, 3, 2):
            for i in (0, 1):
                mine(e, i).wait_recv()
            mates(e).start()
        all_rows().wait_recv()
        choose_all()
        correlate(0, 0)
        correlate(0, 2)
        for f in fars:
            for pair in ((0, 1), (2, 3)):
                for e in pair:
                    for i in (1, 0):
                        inside(f, e, i).wait_recv()
                correlate(f, pair[0])
        inside(0, 0, 0).wait_send()
        for f in fars:
            far(f, 0, me).wait_send()
        for e in (1, 3, 2):
            mine(e, 0).wait_send()
            mates(e).wait_send()

    @pl.when(core == 1)
    def _():
        pl.semaphore_wait(barrier, n + 6)
        for f in fars:
            far(f, 1, me).start()
        for e in (1, 3, 2):
            mine(e, 1).start()
        inside(0, 0, 1).start()
        send_index()
        for f in fars:
            for i in (1, 0):
                far(f, i, me).wait_recv()
                for e in (3, 1, 2):
                    near(f, e, i, chip(f, 0)).start()
                inside(f, 0, i).start()
        inside(0, 0, 0).wait_recv()
        lag_rows()
        for f in fars:
            for e in (1, 2, 3):
                near(f, e, 1, me).wait_recv()
                inside(f, e, 1).start()
        for m in range(1, n):
            index_to(m).wait_recv()
        all_rows().start()
        choose_all()
        mates(1).wait_recv()
        correlate(0, 0)
        for f in fars:
            for e in (1, 2, 3):
                near(f, e, 0, me).wait_recv()
                inside(f, e, 0).start()
            correlate(f, 0)
            correlate(f, 2)
        for e in (3, 2):
            mates(e).wait_recv()
        correlate(0, 2)
        inside(0, 0, 1).wait_send()
        for e in (1, 3, 2):
            mine(e, 1).wait_send()
        for f in fars:
            far(f, 1, me).wait_send()
            for i in (1, 0):
                for e in (1, 2, 3):
                    near(f, e, i, me).wait_send()
                    inside(f, e, i).wait_send()
                inside(f, 0, i).wait_send()
        all_rows().wait_send()
        for m in range(1, n):
            index_to(m).wait_send()


def shards(n, raw, live_index, live_count):
    slots = raw.shape[0]
    vmem = pl.BlockSpec(memory_space=pltpu.VMEM)
    return pl.pallas_call(
        functools.partial(kernel, n),
        out_shape=pltpu.VMEM((L // 2, slots, n * slots), jnp.bfloat16),
        in_specs=[
            pl.BlockSpec(memory_space=pl.ANY),
            pl.BlockSpec(memory_space=pl.ANY),
            pl.BlockSpec(memory_space=pl.ANY),
            pl.BlockSpec(memory_space=pl.ANY),
            pl.BlockSpec(memory_space=pl.ANY),
        ],
        out_specs=vmem,
        scratch_shapes=[
            pltpu.VMEM((1, slots), jnp.int32),
            pltpu.SMEM((n,), jnp.int32),
            pltpu.VMEM((16, COLS), jnp.float32),
            pltpu.VMEM((BASE, COLS + 128), jnp.float32),
            pltpu.VMEM((slots // 2, S), jnp.bfloat16),
            pltpu.VMEM((2 * slots, KROWS), jnp.bfloat16),
            pltpu.VMEM((KROWS, COLS), jnp.bfloat16),
            pltpu.VMEM((2 * slots, COLS), jnp.float32),
            pltpu.VMEM((n * slots, COLS), jnp.bfloat16),
            pltpu.VMEM((L // 2 * slots, COLS), jnp.bfloat16),
            pltpu.VMEM((n, 1, slots), jnp.int32),
            pltpu.VMEM((n // 2, 2 * slots, 2 * slots), jnp.bfloat16),
            pltpu.SemaphoreType.DMA,
            pltpu.SemaphoreType.DMA((3,)),
            pltpu.SemaphoreType.DMA,
            pltpu.SemaphoreType.DMA((n // 2,)),
            pltpu.SemaphoreType.DMA((n // 2,)),
            pltpu.SemaphoreType.DMA((2 * n,)),
            pltpu.SemaphoreType.DMA((2 * n,)),
            pltpu.SemaphoreType.DMA((2 * n,)),
            pltpu.SemaphoreType.DMA((2 * n,)),
            pltpu.SemaphoreType.DMA((n,)),
            pltpu.SemaphoreType.DMA((n,)),
        ],
        compiler_params=pltpu.CompilerParams(
            collective_id=0, has_side_effects=True, vmem_limit_bytes=VMEM_LIMIT - 6 * slots * n * slots
        ),
    )(
        raw.reshape(slots, S),
        live_index,
        live_count,
        jnp.asarray(dft_table(), jnp.bfloat16),
        jnp.asarray(lag_table()),
    )


def solution(mesh):
    return jax.shard_map(
        functools.partial(shards, mesh.shape["chan"]),
        mesh=mesh,
        in_specs=(P(("groups", "chan"), None, None), P(("groups", "chan"), None), P("groups")),
        out_specs=P("pair", ("groups", "chan"), None),
        check_vma=False,
    )
```
